512 devices in a mesh: pw: 32 (over z, x_hi, core), band: 16 (over x_lo, y).
Axes of the slice: x: 4 (x_hi: 2, x_lo: 2; x = x_hi * 2 + x_lo), y: 8, z: 8, core: 2. Of those that a mesh axis runs over, the one named last changes fastest.
Arguments:
- wavefunctions: bfloat16 [2, 16384, 2048], P(None, 'pw', 'band'), may hold values from -0.046875 to 0.046875
- miller: int32 [3, 16384], P(None, 'pw'), may hold values from -16 to 16
- reciprocal: float32 [3, 3], replicated, may hold values from -0.15 to 1.15, as said below
- fractional: float32 [3, 128], replicated, may hold values from 0 to 1
- species: int32 [128], replicated, may hold values from 0 to 3
- atom_order: int32 [128], replicated, may hold values from 0 to 127, each once
- radial_widths: float32 [4, 4], replicated, may hold values from 0.003 to 0.02
- onsite_base: float32 [4, 8, 8], replicated, may hold values from -2 to 2
- coupling: float32 [4, 64, 64], replicated, may hold values from -0.75 to 0.75
- occupations: float32 [2048], P('band'), may hold values from 0 to 3, as said below
Outputs:
- applied: bfloat16 [2, 16384, 2048], P(None, 'pw', 'band')
- onsite_d: float32 [128, 8, 8], P('pw')
The draws below stay inside these ranges and needn't reach their ends.
Inputs may be any that keep to these rules, and one draw needn't show every extreme that they name: `atom_order`: a permutation of the atoms. `reciprocal`: each diagonal entry is 0.85 or more and each other entry 0.15 or less in magnitude. `occupations`: positive.
All inputs are finite; a program needn't handle non-finite values.
Results may differ from the reference program's by a relative error of at most 0.008.
Values may be sent and summed in bfloat16 or wider, within the bound.
No kernel may reach another device: no remote copies, remote signals or barrier semaphores. Data moves between devices by JAX's collectives and lax.ppermute only.
A program may use at most 64 MiB of HBM per device.

```python
import math
import jax
import jax.numpy as jnp
from jax import lax

PROJ = 8
SPECIES = 4
NPW = 16384
NBANDS = 2048
ATOMS = 128


def draw_occupations(key, part):
    position = jnp.arange(NBANDS, dtype=jnp.float32) / NBANDS
    fermi = 2.0 / (1.0 + jnp.exp((position - 0.8) * 6.0))
    noise = jax.random.uniform(key, (NBANDS,), jnp.float32, 0.8, 1.2)
    return fermi * noise


def draw_reciprocal(key, part):
    offsets = 0.05 * jax.random.truncated_normal(key, -3.0, 3.0, (3, 3), jnp.float32)
    return jnp.eye(3, dtype=jnp.float32) + offsets


def set_ends(drawn, key, least, largest):
    shape = drawn.shape
    index_at = [jax.random.randint(jax.random.fold_in(key, axis), (), 0, shape[axis]) for axis in range(len(shape))]
    drawn = drawn.at[tuple(index_at)].set(least)
    longest = shape.index(max(shape))
    index_at[longest] = (index_at[longest] + 1) % shape[longest]
    return drawn.at[tuple(index_at)].set(largest)


def levels(stream_key, extent, split, low, high):
    loudness, own = 1.0, jax.random.fold_in(stream_key, 6)
    for dim, parts in split:
        steps = jnp.exp(jax.random.uniform(jax.random.fold_in(own, dim), (parts,), jnp.float32, low / len(split), high / len(split)))
        loudness = loudness * jnp.repeat(steps, extent[dim] // parts).reshape([-1 if axis == dim else 1 for axis in range(len(extent))])
    return loudness


def scatter_about(own_key, shape, deviation, bound, pieces=(), kind=jnp.bfloat16):
    factor_of = levels(own_key, shape, pieces, -0.22, 0.18) if pieces else 1.0
    values = jax.random.normal(own_key, shape, jnp.float32) * deviation * factor_of
    return jnp.minimum(jnp.maximum(values, -bound), bound).astype(kind)


def setup_inputs(seed: int = 0) -> dict:
    arg_keys = jax.random.split(jax.random.key(seed), 11)
    wavefunctions = scatter_about(arg_keys[0], (2, NPW, NBANDS), NPW ** -0.5, 0.046875, ((1, 32), (2, 16)))
    miller = set_ends(jax.random.randint(arg_keys[1], (3, NPW), -16, 17), jax.random.fold_in(arg_keys[1], 1), -16, 16).astype(jnp.int32)
    reciprocal = draw_reciprocal(jax.random.fold_in(arg_keys[10], 71), 0)
    fractional = jnp.clip(jax.random.uniform(arg_keys[3], (3, ATOMS), jnp.float32, 0.0, 1.0), 0.0, 1.0)
    species = set_ends(jax.random.randint(arg_keys[4], (ATOMS,), 0, SPECIES), jax.random.fold_in(arg_keys[4], 1), 0, SPECIES - 1).astype(jnp.int32)
    atom_order = jax.random.permutation(arg_keys[5], ATOMS).astype(jnp.int32)
    radial_widths = jnp.clip(jnp.exp(jax.random.uniform(arg_keys[6], (SPECIES, 4), jnp.float32, math.log(0.003), math.log(0.02))), 0.003, 0.02)
    onsite_base = scatter_about(arg_keys[7], (SPECIES, PROJ, PROJ), PROJ ** -0.5, 2.0, (), jnp.float32)
    coupling = scatter_about(arg_keys[8], (SPECIES, PROJ * PROJ, PROJ * PROJ), (PROJ * PROJ) ** -0.5, 0.75, (), jnp.float32)
    occupations = draw_occupations(jax.random.fold_in(arg_keys[10], 71), 0)
    return {"wavefunctions": wavefunctions, "miller": miller, "reciprocal": reciprocal, "fractional": fractional, "species": species, "atom_order": atom_order, "radial_widths": radial_widths, "onsite_base": onsite_base, "coupling": coupling, "occupations": occupations}


HIGH = lax.Precision.HIGHEST


def projector_tile(miller_cols, reciprocal, positions, atom_species, radial_widths):
    two_pi = 2.0 * math.pi
    miller_real = miller_cols.astype(jnp.float32)
    g_vectors = two_pi * jnp.dot(reciprocal, miller_real, precision=HIGH)
    g_square = jnp.sum(g_vectors * g_vectors, axis=0)
    phases = two_pi * jnp.dot(positions.T, miller_real, precision=HIGH)
    onehot = (atom_species[:, None] == jnp.arange(radial_widths.shape[0], dtype=jnp.int32)[None, :]).astype(jnp.float32)
    widths = jnp.dot(onehot, radial_widths, precision=HIGH)
    radial = jnp.exp(-0.5 * g_square[None, None, :] * (widths * widths)[:, :, None])
    s_part = radial[:, 0:2, :]
    p_first = g_vectors[None, :, :] * (widths[:, 2, None, None] * radial[:, 2:3, :])
    p_second = g_vectors[None, :, :] * (widths[:, 3, None, None] * radial[:, 3:4, :])
    p_part = jnp.concatenate([p_first, p_second], axis=1)
    cosine = jnp.cos(phases)[:, None, :]
    sine = jnp.sin(phases)[:, None, :]
    beta_real = jnp.concatenate([s_part * cosine, -p_part * sine], axis=1)
    beta_imag = jnp.concatenate([-s_part * sine, -p_part * cosine], axis=1)
    rows = positions.shape[1] * 8
    return (beta_real.reshape(rows, -1).astype(jnp.bfloat16), beta_imag.reshape(rows, -1).astype(jnp.bfloat16))


def project(beta_real, beta_imag, wave_real, wave_imag):
    proj_real = jnp.dot(beta_real, wave_real, preferred_element_type=jnp.float32) + jnp.dot(beta_imag, wave_imag, preferred_element_type=jnp.float32)
    proj_imag = jnp.dot(beta_real, wave_imag, preferred_element_type=jnp.float32) - jnp.dot(beta_imag, wave_real, preferred_element_type=jnp.float32)
    return jnp.stack([proj_real, proj_imag], axis=1)


def occupancy_terms(projections, weights):
    grouped = projections.reshape(projections.shape[0] // 8, 8, 2, projections.shape[2])
    return jnp.einsum("aicn,ajcn,n->aij", grouped, grouped, weights, precision=HIGH)


def onsite_matrix(occupancy, atom_species, onsite_base, coupling):
    count = occupancy.shape[0]
    kinds = onsite_base.shape[0]
    onehot = (atom_species[:, None] == jnp.arange(kinds, dtype=jnp.int32)[None, :]).astype(jnp.float32)
    response = jnp.einsum("skl,al->ask", coupling, occupancy.reshape(count, 64), precision=HIGH)
    base = jnp.einsum("as,sk->ak", onehot, onsite_base.reshape(kinds, 64), precision=HIGH)
    total = base + jnp.einsum("as,ask->ak", onehot, response, precision=HIGH)
    return total.reshape(count, 8, 8)


def weigh(onsite, projections):
    grouped = projections.reshape(projections.shape[0] // 8, 8, 2, projections.shape[2])
    weighted = jnp.einsum("aij,ajcn->aicn", onsite, grouped, precision=HIGH)
    return weighted.reshape(projections.shape).astype(jnp.bfloat16)


def back_project(beta_real, beta_imag, weighted):
    dims = (((0,), (0,)), ((), ()))
    q_real = weighted[:, 0, :]
    q_imag = weighted[:, 1, :]
    out_real = lax.dot_general(beta_real, q_real, dims, preferred_element_type=jnp.float32) - lax.dot_general(beta_imag, q_imag, dims, preferred_element_type=jnp.float32)
    out_imag = lax.dot_general(beta_real, q_imag, dims, preferred_element_type=jnp.float32) + lax.dot_general(beta_imag, q_real, dims, preferred_element_type=jnp.float32)
    return jnp.stack([out_real, out_imag], axis=0)


def reference(wavefunctions, miller, reciprocal, fractional, species, atom_order, radial_widths, onsite_base, coupling, occupations):
    sorted_species = species[atom_order]
    sorted_positions = fractional[:, atom_order]
    beta_real, beta_imag = projector_tile(miller, reciprocal, sorted_positions, sorted_species, radial_widths)
    projections = project(beta_real, beta_imag, wavefunctions[0], wavefunctions[1])
    weights = occupations / NBANDS
    occupancy = occupancy_terms(projections, weights)
    onsite = onsite_matrix(occupancy, sorted_species, onsite_base, coupling)
    weighted = weigh(onsite, projections)
    applied = back_project(beta_real, beta_imag, weighted).astype(jnp.bfloat16)
    return applied, onsite
```

```python
import math

import jax
import jax.numpy as jnp
from jax import lax
from jax.experimental import pallas as pl
from jax.experimental.pallas import tpu as pltpu
from jax.sharding import Mesh
from jax.sharding import PartitionSpec as P

HIGH = lax.Precision.HIGHEST
F32 = jnp.float32
BF16 = jnp.bfloat16
SIN = (6.283185005187988, -41.341590881347656, 81.59994506835938,
       -76.61447143554688, 41.3428840637207, -12.471243858337402)
COS = (1.0, -19.73920440673828, 64.93911743164062, -85.45014190673828,
       60.16762924194336, -25.967599868774414, 6.528658390045166)
NT = (((1,), (1,)), ((), ()))
NN = (((1,), (0,)), ((), ()))


def dot_high(left, right, dims):
    return lax.dot_general(left, right, dims, precision=HIGH, preferred_element_type=F32)


def iota(shape, dim):
    return lax.broadcasted_iota(jnp.int32, shape, dim)


def horner(coefficients, z):
    total = jnp.full_like(z, coefficients[-1])
    for c in coefficients[-2::-1]:
        total = total * z + c
    return total


def vmem():
    return pl.BlockSpec(memory_space=pltpu.VMEM)


def smem():
    return pl.BlockSpec(memory_space=pltpu.SMEM)


def tables_kernel(core_ref, recip_ref, widths_ref, wave_ref, miller_ref, frac_ref, species_ref,
                  order_ref, beta_ref, proj_ref, rhs_ref):
    core = core_ref[0]
    gcount = miller_ref.shape[1]
    natoms = order_ref.shape[1]
    owners = beta_ref.shape[0] // 32
    kinds = widths_ref.shape[0]
    spec = species_ref[...]
    rows = [frac_ref[d:d + 1, :] for d in range(3)]
    for c in range(4):
        row = jnp.zeros((1, natoms), F32)
        for s in range(kinds):
            row = jnp.where(spec == s, widths_ref[s, c], row)
        rows.append(row)
    rows.append(jnp.zeros((1, natoms), F32))
    by_atom = jnp.concatenate(rows, axis=0)
    pick = (iota((natoms, natoms), 0) == order_ref[...]).astype(F32)
    by_slot = dot_high(by_atom, pick, NN)
    row_id = iota((owners * 8, natoms), 0)
    slot = (row_id // 8) * 8 + core * 4 + row_id % 4
    expand = (iota((owners * 8, natoms), 1) == slot).astype(F32)
    by_row = dot_high(expand, by_slot, NT)

    mil = miller_ref[...].astype(F32)
    m = [mil[d:d + 1, :] for d in range(3)]
    two_pi = 2.0 * math.pi
    g = [two_pi * (recip_ref[d, 0] * m[0] + recip_ref[d, 1] * m[1] + recip_ref[d, 2] * m[2]) for d in range(3)]
    g2 = g[0] * g[0] + g[1] * g[1] + g[2] * g[2]
    wide = (8, gcount)
    m = [jnp.broadcast_to(a, wide) for a in m]
    g2 = jnp.broadcast_to(g2, wide)
    g = [jnp.broadcast_to(a, wide) for a in g]
    first = iota(wide, 0) < 4
    pair_g = (None, jnp.where(first, g[0], g[1]), jnp.where(first, g[2], g[0]), jnp.where(first, g[1], g[2]))
    first1 = iota((8, 1), 0) < 4

    for q in range(owners):
        par = by_row[q * 8:q * 8 + 8, :]
        col = [par[:, k:k + 1] for k in range(7)]
        turns = col[0] * m[0] + col[1] * m[1] + col[2] * m[2]
        r = turns - jnp.round(turns)
        z = r * r
        sin = horner(SIN, z) * r
        cos = horner(COS, z)
        minus_sin = -sin
        pair_w = (jnp.where(first1, col[3], col[4]), col[5], jnp.where(first1, col[5], col[6]), col[6])
        re, im = [], []
        for p in range(4):
            w = pair_w[p]
            decay = jnp.exp(g2 * (-0.5 * (w * w)))
            if p == 0:
                re.append(decay * cos)
                im.append(decay * minus_sin)
            else:
                amp = pair_g[p] * ((-w) * decay)
                re.append(amp * sin)
                im.append(amp * cos)
        beta_ref[q * 32:q * 32 + 32, 0:gcount] = jnp.concatenate(re, axis=0).astype(BF16)
        beta_ref[q * 32:q * 32 + 32, gcount:] = jnp.concatenate(im, axis=0).astype(BF16)

    nb = wave_ref.shape[2]
    real, imag = wave_ref[0], wave_ref[1]
    rhs_ref[0:gcount, 0:nb] = real
    rhs_ref[0:gcount, nb:] = imag
    rhs_ref[gcount:, 0:nb] = imag
    rhs_ref[gcount:, nb:] = -real
    proj_ref[...] = jnp.dot(beta_ref[...], rhs_ref[...], preferred_element_type=F32).astype(proj_ref.dtype)


def tables(core, kind, wavefunctions, miller, reciprocal, fractional, species, atom_order, radial_widths):
    gcount, nb = wavefunctions.shape[1:]
    nrows = atom_order.shape[1] * 4
    return pl.pallas_call(
        tables_kernel,
        out_shape=(jax.ShapeDtypeStruct((nrows, 2 * gcount), BF16), jax.ShapeDtypeStruct((nrows, 2 * nb), kind)),
        in_specs=[smem(), smem(), smem()] + [vmem()] * 5,
        out_specs=(vmem(), vmem()),
        scratch_shapes=[pltpu.VMEM((2 * gcount, 2 * nb), BF16)],
        compiler_params=pltpu.CompilerParams(vmem_limit_bytes=32 << 20),
        name="tables",
    )(core, reciprocal, radial_widths, wavefunctions, miller, fractional, species, atom_order)


def prepare_kernel(owner_ref, species_ref, order_ref, mine_ref, other_ref, coupling_ref, base_ref,
                   mine_t_ref, other_t_ref, couple_ref, base_rows_ref):
    for src, dst in ((mine_ref, mine_t_ref), (other_ref, other_t_ref)):
        nrows, width = src.shape[0], src.shape[1] // 2
        for part in range(2):
            block = src[:, part * width:(part + 1) * width]
            dst[:, part * nrows:(part + 1) * nrows] = block.T
    row = iota((32, 64), 0) % 4
    base = jnp.zeros((32, 64), F32)
    for a in range(4):
        s = species_ref[order_ref[owner_ref[0] * 4 + a]]
        couple_ref[:, a * 64:(a + 1) * 64] = coupling_ref[s]
        base = jnp.where(row == a, base_ref[pl.ds(s, 1), :], base)
    base_rows_ref[...] = base


def prepare(owner, species, atom_order, mine, other, coupling, base):
    nrows, width = mine.shape
    turned = jax.ShapeDtypeStruct((width // 2, 2 * nrows), BF16)
    return pl.pallas_call(
        prepare_kernel,
        out_shape=(turned, turned, jax.ShapeDtypeStruct((64, 256), F32), jax.ShapeDtypeStruct((32, 64), F32)),
        in_specs=[smem(), smem(), smem()] + [vmem()] * 4,
        out_specs=(vmem(),) * 4,
        compiler_params=pltpu.CompilerParams(vmem_limit_bytes=32 << 20),
        name="prepare",
    )(owner, species, atom_order, mine, other, coupling, base)


def occupancy_kernel(parts_ref, weights_ref, proj_ref, send_ref):
    total = parts_ref[0].astype(F32)
    for k in range(1, parts_ref.shape[0]):
        total = total + parts_ref[k].astype(F32)
    proj_ref[...] = total
    w = weights_ref[...]
    gram = dot_high(total * jnp.concatenate([w, w], axis=1), total, NT)
    gram = jnp.where(iota((32, 32), 0) % 4 == iota((32, 32), 1) % 4, gram, 0.0)
    lane = iota((32, 128), 1)
    spread = (iota((32, 128), 0) // 4 == lane % 8).astype(F32)
    wide = dot_high(gram, spread, NN)
    row = iota((32, 128), 0)
    wide = jnp.where(((lane // 8) % 8 == row // 4) & (lane // 64 == (row % 4) % 2), wide, 0.0)
    fold = ((iota((8, 32), 1) % 4) // 2 == iota((8, 32), 0)).astype(F32)
    flat = dot_high(fold, wide, NN)[0:2, :]
    for k in range(send_ref.shape[0]):
        send_ref[k] = flat


def occupancy_step(parts, weights, peers):
    _, nrows, width = parts.shape
    return pl.pallas_call(
        occupancy_kernel,
        out_shape=(jax.ShapeDtypeStruct((nrows, width), F32), jax.ShapeDtypeStruct((peers, 2, 128), F32)),
        in_specs=[vmem(), vmem()],
        out_specs=(vmem(), vmem()),
        name="occupancy",
    )(parts, weights)


def weigh_kernel(parts_ref, proj_ref, couple_ref, base_ref, onsite_ref, send_ref):
    occ = jnp.sum(parts_ref[...], axis=0)
    flat = jnp.concatenate([occ[0:1, :], occ[1:2, :]], axis=1)
    lane = iota((32, 256), 1)
    by_atom = jnp.where(lane // 64 == iota((32, 256), 0) % 4, flat, 0.0)
    onsite = dot_high(by_atom, couple_ref[...], NT) + base_ref[...]
    onsite_ref[...] = onsite[0:4, :]
    row = iota((32, 64), 0)
    onsite = jnp.where(iota((32, 64), 1) // 8 == row // 4, onsite, 0.0)
    spread = (iota((64, 32), 0) % 8 == iota((64, 32), 1) // 4).astype(F32)
    full = dot_high(onsite, spread, NN)
    full = jnp.where(iota((32, 32), 0) % 4 == iota((32, 32), 1) % 4, full, 0.0)
    weighted = dot_high(full, proj_ref[...], NN).astype(BF16)
    for k in range(send_ref.shape[0]):
        send_ref[k] = weighted


def weigh(parts, proj, couple, base_rows, peers):
    return pl.pallas_call(
        weigh_kernel,
        out_shape=(jax.ShapeDtypeStruct((4, 64), F32), jax.ShapeDtypeStruct((peers, *proj.shape), BF16)),
        in_specs=[vmem()] * 4,
        out_specs=(vmem(), vmem()),
        name="weigh",
    )(parts, proj, couple, base_rows)


def product_with(table_ref, weighted_ref):
    nrows, width = weighted_ref.shape
    real, imag = weighted_ref[:, :width // 2], weighted_ref[:, width // 2:]
    turned = jnp.concatenate([-imag, real], axis=1)
    return (jnp.dot(table_ref[:, :nrows], weighted_ref[...], preferred_element_type=F32)
            + jnp.dot(table_ref[:, nrows:], turned, preferred_element_type=F32))


def back_kernel(table_ref, weighted_ref, out_ref):
    out_ref[...] = product_with(table_ref, weighted_ref)


def back_last_kernel(table_ref, weighted_ref, before_ref, out_ref):
    total = before_ref[...] + product_with(table_ref, weighted_ref)
    half = total.shape[1] // 2
    out_ref[0] = total[:, :half].astype(BF16)
    out_ref[1] = total[:, half:].astype(BF16)


def back_project(table, weighted, before=None):
    gcount, width = table.shape[0], weighted.shape[1]
    if before is None:
        return pl.pallas_call(
            back_kernel,
            out_shape=jax.ShapeDtypeStruct((gcount, width), F32),
            in_specs=[vmem()] * 2, out_specs=vmem(), name="back",
        )(table, weighted)
    return pl.pallas_call(
        back_last_kernel,
        out_shape=jax.ShapeDtypeStruct((2, gcount, width // 2), BF16),
        in_specs=[vmem()] * 3, out_specs=vmem(), name="back_last",
    )(table, weighted, before)


def local(wavefunctions, miller, reciprocal, fractional, species, atom_order, radial_widths,
          onsite_base, coupling, occupations):
    chips = lax.axis_size("chip")
    bands = lax.axis_size("band")
    core = lax.axis_index("core")
    owner = lax.axis_index("chip") * 2 + core
    swap = [(0, 1), (1, 0)]
    nb = wavefunctions.shape[2]
    args = (wavefunctions, miller, reciprocal, fractional, species.reshape(1, -1), atom_order.reshape(1, -1),
            radial_widths)
    other, other_proj = tables((1 - core).reshape(1), BF16, *args)
    received = lax.ppermute(other_proj, "core", swap)
    mine, mine_proj = tables(core.reshape(1), F32, *args)
    chip_sum = (mine_proj + received.astype(F32)).astype(BF16).reshape(chips, -1, 2 * nb)
    parts = lax.all_to_all(chip_sum, "chip", 0, 0, tiled=True)
    mine_t, other_t, couple, base_rows = prepare(
        owner.reshape(1), species, atom_order, mine, other, coupling, onsite_base.reshape(-1, 64))

    weights = (occupations / (nb * bands)).reshape(1, -1)
    proj, occupancy = occupancy_step(parts, weights, bands)
    occupancy = lax.all_to_all(occupancy, "band", 0, 0, tiled=True)
    onsite, weighted = weigh(occupancy, proj, couple, base_rows, chips)
    weighted = lax.all_to_all(weighted, "chip", 0, 0, tiled=True).reshape(-1, 2 * nb)
    other_weighted = lax.ppermute(weighted, "core", swap)
    applied = back_project(mine_t, weighted)
    applied = back_project(other_t, other_weighted, applied)
    return applied, onsite.reshape(-1, 8, 8)


def solution(mesh):
    peers, bands = mesh.devices.shape
    inner = Mesh(mesh.devices.reshape(peers // 2, 2, bands), ("chip", "core", "band"))
    pw = ("chip", "core")
    placed = (P(None, pw, "band"), P(None, pw), P(), P(), P(), P(), P(), P(), P(), P("band"))
    return jax.shard_map(
        local,
        mesh=inner,
        in_specs=placed,
        out_specs=(P(None, pw, "band"), P(pw, None, None)),
        check_vma=False,
    )
```

```python
import functools
import math

import jax
import jax.numpy as jnp
from jax import lax
from jax.experimental import pallas as pl
from jax.experimental.pallas import tpu as pltpu
from jax.sharding import Mesh
from jax.sharding import PartitionSpec as P

HIGH = lax.Precision.HIGHEST
F32 = jnp.float32
BF16 = jnp.bfloat16
SIN = (6.283185005187988, -41.341590881347656, 81.59994506835938,
       -76.61447143554688, 41.3428840637207, -12.471243858337402)
COS = (1.0, -19.73920440673828, 64.93911743164062, -85.45014190673828,
       60.16762924194336, -25.967599868774414, 6.528658390045166)
NT = (((1,), (1,)), ((), ()))
TN = (((0,), (0,)), ((), ()))
NN = (((1,), (0,)), ((), ()))


LIMIT = pltpu.CompilerParams(vmem_limit_bytes=16 << 20)


def dot_high(left, right, dims):
    return lax.dot_general(left, right, dims, precision=HIGH, preferred_element_type=F32)


def iota(shape, dim):
    return lax.broadcasted_iota(jnp.int32, shape, dim)


def horner(coefficients, z):
    total = jnp.full_like(z, coefficients[-1])
    for c in coefficients[-2::-1]:
        total = total * z + c
    return total


def vmem():
    return pl.BlockSpec(memory_space=pltpu.VMEM)


def smem():
    return pl.BlockSpec(memory_space=pltpu.SMEM)


def tables_kernel(core_ref, recip_ref, widths_ref, wave_hbm, miller_ref, frac_ref, species_ref,
                  order_ref, beta_ref, proj_ref, wave_ref, rhs_ref, copied):
    load = pltpu.make_async_copy(wave_hbm, wave_ref, copied)
    load.start()
    core = core_ref[0]
    gcount = miller_ref.shape[1]
    natoms = order_ref.shape[1]
    owners = beta_ref.shape[0] // 32
    kinds = widths_ref.shape[0]
    spec = species_ref[...]
    rows = [frac_ref[d:d + 1, :] for d in range(3)]
    for c in range(4):
        row = jnp.zeros((1, natoms), F32)
        for s in range(kinds):
            row = jnp.where(spec == s, widths_ref[s, c], row)
        rows.append(row)
    rows.append(jnp.zeros((1, natoms), F32))
    by_atom = jnp.concatenate(rows, axis=0)
    pick = (iota((natoms, natoms), 0) == order_ref[...]).astype(F32)
    by_slot = dot_high(by_atom, pick, NN)
    row_id = iota((owners * 8, natoms), 0)
    slot = (row_id // 8) * 8 + core * 4 + row_id % 4
    expand = (iota((owners * 8, natoms), 1) == slot).astype(F32)
    by_row = dot_high(expand, by_slot, NT)

    mil = miller_ref[...].astype(F32)
    m = [mil[d:d + 1, :] for d in range(3)]
    two_pi = 2.0 * math.pi
    g = [two_pi * (recip_ref[d, 0] * m[0] + recip_ref[d, 1] * m[1] + recip_ref[d, 2] * m[2]) for d in range(3)]
    g2 = g[0] * g[0] + g[1] * g[1] + g[2] * g[2]
    wide = (8, gcount)
    m = [jnp.broadcast_to(a, wide) for a in m]
    g2 = jnp.broadcast_to(g2, wide)
    g = [jnp.broadcast_to(a, wide) for a in g]
    first = iota(wide, 0) < 4
    pair_g = (None, jnp.where(first, g[0], g[1]), jnp.where(first, g[2], g[0]), jnp.where(first, g[1], g[2]))
    first1 = iota((8, 1), 0) < 4

    for q in range(owners):
        par = by_row[q * 8:q * 8 + 8, :]
        col = [par[:, k:k + 1] for k in range(7)]
        turns = col[0] * m[0] + col[1] * m[1] + col[2] * m[2]
        r = turns - jnp.round(turns)
        z = r * r
        sin = horner(SIN, z) * r
        cos = horner(COS, z)
        minus_sin = -sin
        pair_w = (jnp.where(first1, col[3], col[4]), col[5], jnp.where(first1, col[5], col[6]), col[6])
        re, im = [], []
        for p in range(4):
            w = pair_w[p]
            decay = jnp.exp(g2 * (-0.5 * (w * w)))
            if p == 0:
                re.append(decay * cos)
                im.append(decay * minus_sin)
            else:
                amp = pair_g[p] * ((-w) * decay)
                re.append(amp * sin)
                im.append(amp * cos)
        beta_ref[q * 32:q * 32 + 32, 0:gcount] = jnp.concatenate(re, axis=0).astype(BF16)
        beta_ref[q * 32:q * 32 + 32, gcount:] = jnp.concatenate(im, axis=0).astype(BF16)

    load.wait()
    nb = wave_ref.shape[2]
    real, imag = wave_ref[0], wave_ref[1]
    rhs_ref[0:gcount, 0:nb] = real
    rhs_ref[0:gcount, nb:] = imag
    rhs_ref[gcount:, 0:nb] = imag
    rhs_ref[gcount:, nb:] = -real
    proj_ref[...] = jnp.dot(beta_ref[...], rhs_ref[...], preferred_element_type=F32).astype(proj_ref.dtype)


def own_tables_kernel(bands, core_ref, recip_ref, widths_ref, wave_hbm, miller_ref, frac_ref, species_ref,
                      order_ref, owner_ref, species_smem, order_smem, coupling_ref, base_ref, occupations_ref,
                      beta_ref, proj_ref, couple_ref, base_rows_ref, weights_ref, wave_ref, rhs_ref, copied):
    tables_kernel(core_ref, recip_ref, widths_ref, wave_hbm, miller_ref, frac_ref, species_ref, order_ref,
                  beta_ref, proj_ref, wave_ref, rhs_ref, copied)
    row = iota((32, 64), 0) % 4
    base = jnp.zeros((32, 64), F32)
    for a in range(4):
        s = species_smem[order_smem[owner_ref[0] * 4 + a]]
        couple_ref[:, a * 64:(a + 1) * 64] = coupling_ref[s]
        base = jnp.where(row == a, base_ref[pl.ds(s, 1), :], base)
    base_rows_ref[...] = base
    w = occupations_ref[...] * (1.0 / (occupations_ref.shape[1] * bands))
    weights_ref[...] = jnp.concatenate([w, w], axis=1)


def tables(core, wavefunctions, miller, reciprocal, fractional, species, atom_order, radial_widths, own=None):
    gcount, nb = wavefunctions.shape[1:]
    nrows = atom_order.shape[0] * 4
    kind = BF16 if own is None else F32
    body, more, more_specs = tables_kernel, (), []
    outs = [jax.ShapeDtypeStruct((nrows, 2 * gcount), BF16), jax.ShapeDtypeStruct((nrows, 2 * nb), kind)]
    if own is not None:
        bands, owner, coupling, base, occupations = own
        body = functools.partial(own_tables_kernel, bands)
        more = (owner, species, atom_order, coupling, base, occupations)
        more_specs = [smem()] * 3 + [vmem()] * 3
        outs += [jax.ShapeDtypeStruct((64, 256), F32), jax.ShapeDtypeStruct((32, 64), F32),
                 jax.ShapeDtypeStruct((1, 2 * nb), F32)]
    return pl.pallas_call(
        body,
        out_shape=tuple(outs),
        in_specs=[smem()] * 3 + [pl.BlockSpec(memory_space=pltpu.HBM)] + [vmem()] * 4 + more_specs,
        out_specs=(vmem(),) * len(outs),
        scratch_shapes=[pltpu.VMEM((2, gcount, nb), BF16), pltpu.VMEM((2 * gcount, 2 * nb), BF16),
                        pltpu.SemaphoreType.DMA],
        compiler_params=LIMIT,
        name="tables" if own is None else "own_tables",
    )(core, reciprocal, radial_widths, pltpu.with_memory_space_constraint(wavefunctions, pltpu.HBM), miller,
      fractional, species.reshape(1, -1), atom_order.reshape(1, -1), *more)


def occupancy_kernel(parts_ref, weights_ref, proj_ref, send_ref):
    total = parts_ref[0].astype(F32)
    for k in range(1, parts_ref.shape[0]):
        total = total + parts_ref[k].astype(F32)
    proj_ref[...] = total
    gram = dot_high(total * weights_ref[...], total, NT)
    gram = jnp.where(iota((32, 32), 0) % 4 == iota((32, 32), 1) % 4, gram, 0.0)
    lane = iota((32, 128), 1)
    spread = (iota((32, 128), 0) // 4 == lane % 8).astype(F32)
    wide = dot_high(gram, spread, NN)
    row = iota((32, 128), 0)
    wide = jnp.where(((lane // 8) % 8 == row // 4) & (lane // 64 == (row % 4) % 2), wide, 0.0)
    fold = ((iota((8, 32), 1) % 4) // 2 == iota((8, 32), 0)).astype(F32)
    flat = dot_high(fold, wide, NN)[0:2, :]
    for k in range(send_ref.shape[0]):
        send_ref[k] = flat


def occupancy_step(parts, weights, peers):
    _, nrows, width = parts.shape
    return pl.pallas_call(
        occupancy_kernel,
        out_shape=(jax.ShapeDtypeStruct((nrows, width), F32), jax.ShapeDtypeStruct((peers, 2, 128), F32)),
        in_specs=[vmem(), vmem()],
        out_specs=(vmem(), vmem()),
        compiler_params=LIMIT,
        name="occupancy",
    )(parts, weights)


def weigh_kernel(parts_ref, proj_ref, couple_ref, base_ref, onsite_ref, send_ref):
    occ = jnp.sum(parts_ref[...], axis=0)
    flat = jnp.concatenate([occ[0:1, :], occ[1:2, :]], axis=1)
    lane = iota((32, 256), 1)
    by_atom = jnp.where(lane // 64 == iota((32, 256), 0) % 4, flat, 0.0)
    onsite = dot_high(by_atom, couple_ref[...], NT) + base_ref[...]
    row = iota((32, 64), 0)
    onsite = jnp.where(iota((32, 64), 1) // 8 == row // 4, onsite, 0.0)
    spread = (iota((64, 32), 0) % 8 == iota((64, 32), 1) // 4).astype(F32)
    fold = (iota((64, 8), 0) % 8 == iota((64, 8), 1)).astype(F32)
    square = dot_high(onsite, fold, NN)
    for i in range(8):
        onsite_ref[:, i, :] = square[i * 4:i * 4 + 4, :]
    full = dot_high(onsite, spread, NN)
    full = jnp.where(iota((32, 32), 0) % 4 == iota((32, 32), 1) % 4, full, 0.0)
    weighted = dot_high(full, proj_ref[...], NN).astype(BF16)
    for k in range(send_ref.shape[0]):
        send_ref[k] = weighted


def weigh(parts, proj, couple, base_rows, peers):
    return pl.pallas_call(
        weigh_kernel,
        out_shape=(jax.ShapeDtypeStruct((4, 8, 8), F32), jax.ShapeDtypeStruct((peers, *proj.shape), BF16)),
        in_specs=[vmem()] * 4,
        out_specs=(vmem(), vmem()),
        compiler_params=LIMIT,
        name="weigh",
    )(parts, proj, couple, base_rows)


def product_with(table_ref, weighted_ref):
    width = weighted_ref.shape[1]
    gcount = table_ref.shape[1] // 2
    real, imag = weighted_ref[:, :width // 2], weighted_ref[:, width // 2:]
    turned = jnp.concatenate([-imag, real], axis=1)
    return (lax.dot_general(weighted_ref[...], table_ref[:, :gcount], TN, preferred_element_type=F32)
            + lax.dot_general(turned, table_ref[:, gcount:], TN, preferred_element_type=F32))


def back_kernel(table_ref, weighted_ref, out_ref):
    out_ref[...] = product_with(table_ref, weighted_ref)


def back_last_kernel(table_ref, weighted_ref, before_ref, out_ref):
    total = before_ref[...] + product_with(table_ref, weighted_ref)
    half = total.shape[0] // 2
    out_ref[0] = total[:half].T.astype(BF16)
    out_ref[1] = total[half:].T.astype(BF16)


def back_project(table, weighted, before=None):
    gcount, width = table.shape[1] // 2, weighted.shape[1]
    if before is None:
        return pl.pallas_call(
            back_kernel,
            out_shape=jax.ShapeDtypeStruct((width, gcount), F32),
            in_specs=[vmem()] * 2, out_specs=vmem(), compiler_params=LIMIT, name="back",
        )(table, weighted)
    return pl.pallas_call(
        back_last_kernel,
        out_shape=jax.ShapeDtypeStruct((2, gcount, width // 2), BF16),
        in_specs=[vmem()] * 3, out_specs=vmem(), compiler_params=LIMIT, name="back_last",
    )(table, weighted, before)


def local(wavefunctions, miller, reciprocal, fractional, species, atom_order, radial_widths,
          onsite_base, coupling, occupations):
    chips = lax.axis_size("chip")
    bands = lax.axis_size("band")
    core = lax.axis_index("core")
    owner = lax.axis_index("chip") * 2 + core
    swap = [(0, 1), (1, 0)]
    nb = wavefunctions.shape[2]
    args = (wavefunctions, miller, reciprocal, fractional, species, atom_order, radial_widths)
    other, other_proj = tables((1 - core).reshape(1), *args)
    received = lax.ppermute(other_proj, "core", swap)
    own = (bands, owner.reshape(1), coupling, onsite_base.reshape(-1, 64), occupations.reshape(1, -1))
    mine, mine_proj, couple, base_rows, weights = tables(core.reshape(1), *args, own=own)
    chip_sum = (mine_proj + received.astype(F32)).astype(BF16).reshape(chips, -1, 2 * nb)
    parts = lax.all_to_all(chip_sum, "chip", 0, 0, tiled=True)

    proj, occupancy = occupancy_step(parts, weights, bands)
    occupancy = lax.all_to_all(occupancy, "band", 0, 0, tiled=True)
    onsite, weighted = weigh(occupancy, proj, couple, base_rows, chips)
    weighted = lax.all_to_all(weighted, "chip", 0, 0, tiled=True).reshape(-1, 2 * nb)
    other_weighted = lax.ppermute(weighted, "core", swap)
    applied = back_project(mine, weighted)
    applied = back_project(other, other_weighted, applied)
    return applied, onsite


def solution(mesh):
    peers, bands = mesh.devices.shape
    inner = Mesh(mesh.devices.reshape(peers // 2, 2, bands), ("chip", "core", "band"))
    pw = ("chip", "core")
    placed = (P(None, pw, "band"), P(None, pw), P(), P(), P(), P(), P(), P(), P(), P("band"))
    return jax.shard_map(
        local,
        mesh=inner,
        in_specs=placed,
        out_specs=(P(None, pw, "band"), P(pw, None, None)),
        check_vma=False,
    )
```

```python
import functools
import math

import jax
import jax.numpy as jnp
from jax import lax
from jax.experimental import pallas as pl
from jax.experimental.pallas import tpu as pltpu
from jax.sharding import Mesh
from jax.sharding import PartitionSpec as P

HIGH = lax.Precision.HIGHEST
F32 = jnp.float32
BF16 = jnp.bfloat16
SIN = (6.283185005187988, -41.341590881347656, 81.59994506835938,
       -76.61447143554688, 41.3428840637207, -12.471243858337402)
COS = (1.0, -19.73920440673828, 64.93911743164062, -85.45014190673828,
       60.16762924194336, -25.967599868774414, 6.528658390045166)
NT = (((1,), (1,)), ((), ()))
TN = (((0,), (0,)), ((), ()))
NN = (((1,), (0,)), ((), ()))


LIMIT = pltpu.CompilerParams(vmem_limit_bytes=16 << 20)


def dot_high(left, right, dims):
    return lax.dot_general(left, right, dims, precision=HIGH, preferred_element_type=F32)


def iota(shape, dim):
    return lax.broadcasted_iota(jnp.int32, shape, dim)


def horner(coefficients, z):
    total = jnp.full_like(z, coefficients[-1])
    for c in coefficients[-2::-1]:
        total = total * z + c
    return total


def vmem():
    return pl.BlockSpec(memory_space=pltpu.VMEM)


def hbm():
    return pl.BlockSpec(memory_space=pltpu.HBM)


def in_hbm(array):
    return pltpu.with_memory_space_constraint(array, pltpu.HBM)


def fetch(pairs, copied):
    copies = [pltpu.make_async_copy(src, dst, copied.at[k]) for k, (src, dst) in enumerate(pairs)]
    for copy in copies:
        copy.start()
    return copies


def project_rows(by_row, grid_ref, rhs_ref, beta_ref, proj_ref):
    gcount = grid_ref.shape[1]
    wide = (8, gcount)
    m, g = ([jnp.broadcast_to(grid_ref[d:d + 1, :], wide) for d in dims] for dims in ((0, 1, 2), (3, 4, 5)))
    g2 = jnp.broadcast_to(grid_ref[6:7, :], wide)
    first = iota(wide, 0) < 4
    pair_g = (None, jnp.where(first, g[0], g[1]), jnp.where(first, g[2], g[0]), jnp.where(first, g[1], g[2]))
    first1 = iota((8, 1), 0) < 4
    for q in range(by_row.shape[0] // 8):
        par = by_row[q * 8:q * 8 + 8, :]
        col = [par[:, k:k + 1] for k in range(7)]
        turns = col[0] * m[0] + col[1] * m[1] + col[2] * m[2]
        r = turns - jnp.round(turns)
        z = r * r
        sin = horner(SIN, z) * r
        cos = horner(COS, z)
        minus_sin = -sin
        pair_w = (jnp.where(first1, col[3], col[4]), col[5], jnp.where(first1, col[5], col[6]), col[6])
        re, im = [], []
        for p in range(4):
            w = pair_w[p]
            decay = jnp.exp(g2 * (-0.5 * (w * w)))
            if p == 0:
                re.append(decay * cos)
                im.append(decay * minus_sin)
            else:
                amp = pair_g[p] * ((-w) * decay)
                re.append(amp * sin)
                im.append(amp * cos)
        beta_ref[q * 32:q * 32 + 32, 0:gcount] = jnp.concatenate(re, axis=0).astype(BF16)
        beta_ref[q * 32:q * 32 + 32, gcount:] = jnp.concatenate(im, axis=0).astype(BF16)
    proj_ref[...] = jnp.dot(beta_ref[...], rhs_ref[...], preferred_element_type=F32).astype(proj_ref.dtype)


def other_tables_kernel(recip_hbm, widths_hbm, wave_hbm, miller_hbm, frac_hbm, species_hbm, order_hbm,
                        beta_ref, proj_ref, own_row_ref, grid_ref, rhs_ref,
                        recip_ref, widths_ref, wave_ref, miller_ref, frac_ref, species_ref, order_ref, copied):
    loads = fetch(((wave_hbm, wave_ref), (recip_hbm, recip_ref), (widths_hbm, widths_ref), (miller_hbm, miller_ref),
                   (frac_hbm, frac_ref), (species_hbm, species_ref), (order_hbm, order_ref)), copied)
    for load in loads[1:]:
        load.wait()
    core = lax.axis_index("core")
    gcount = miller_ref.shape[1]
    natoms = order_ref.shape[1]
    owners = natoms // 8
    kinds = widths_ref.shape[0]
    spec = species_ref[...]
    rows = [frac_ref[d:d + 1, :] for d in range(3)]
    for c in range(4):
        row = jnp.zeros((1, natoms), F32)
        for s in range(kinds):
            row = jnp.where(spec == s, widths_ref[s:s + 1, c:c + 1], row)
        rows.append(row)
    rows.append(spec.astype(F32))
    by_atom = jnp.concatenate(rows, axis=0)
    pick = (iota((natoms, natoms), 0) == order_ref[...]).astype(F32)
    by_slot = dot_high(by_atom, pick, NN)
    row_id = iota((owners * 16, natoms), 0)
    half = jnp.where(row_id < owners * 8, 1 - core, core)
    slot = ((row_id // 8) % owners) * 8 + half * 4 + row_id % 4
    expand = (iota((owners * 16, natoms), 1) == slot).astype(F32)
    by_row = dot_high(expand, by_slot, NT)
    own_row_ref[...] = by_row[owners * 8:, :]

    mil = miller_ref[...].astype(F32)
    m = [mil[d:d + 1, :] for d in range(3)]
    two_pi = 2.0 * math.pi
    g = [two_pi * (recip_ref[d:d + 1, 0:1] * m[0] + recip_ref[d:d + 1, 1:2] * m[1] + recip_ref[d:d + 1, 2:3] * m[2])
         for d in range(3)]
    g2 = g[0] * g[0] + g[1] * g[1] + g[2] * g[2]
    grid_ref[...] = jnp.concatenate([*m, *g, g2, g2], axis=0)
    loads[0].wait()
    nb = wave_ref.shape[2]
    real, imag = wave_ref[0], wave_ref[1]
    rhs_ref[0:gcount, 0:nb] = real
    rhs_ref[0:gcount, nb:] = imag
    rhs_ref[gcount:, 0:nb] = imag
    rhs_ref[gcount:, nb:] = -real
    project_rows(by_row[:owners * 8, :], grid_ref, rhs_ref, beta_ref, proj_ref)


def other_tables(wavefunctions, miller, reciprocal, fractional, species, atom_order, radial_widths):
    gcount, nb = wavefunctions.shape[1:]
    natoms = atom_order.shape[0]
    args = (reciprocal, radial_widths, wavefunctions, miller, fractional, species.reshape(1, -1),
            atom_order.reshape(1, -1))
    return pl.pallas_call(
        other_tables_kernel,
        out_shape=(jax.ShapeDtypeStruct((natoms * 4, 2 * gcount), BF16),
                   jax.ShapeDtypeStruct((natoms * 4, 2 * nb), BF16),
                   jax.ShapeDtypeStruct((natoms, 8), F32), jax.ShapeDtypeStruct((8, gcount), F32),
                   jax.ShapeDtypeStruct((2 * gcount, 2 * nb), BF16)),
        in_specs=[hbm()] * len(args),
        out_specs=(vmem(),) * 5,
        scratch_shapes=[pltpu.VMEM(a.shape, a.dtype) for a in args] + [pltpu.SemaphoreType.DMA((len(args),))],
        compiler_params=LIMIT,
        name="other_tables",
    )(*(in_hbm(a) for a in args))


def own_tables_kernel(bands, own_row_ref, grid_ref, rhs_ref, base_ref, coupling_hbm, occupations_hbm,
                      beta_ref, proj_ref, couple_ref, base_rows_ref, weights_ref,
                      coupling_ref, occupations_ref, copied):
    loads = fetch(((coupling_hbm, coupling_ref), (occupations_hbm, occupations_ref)), copied)
    project_rows(own_row_ref[...], grid_ref, rhs_ref, beta_ref, proj_ref)
    for load in loads:
        load.wait()
    spec = own_row_ref[pl.ds(pl.multiple_of(lax.axis_index("chip") * 8, 8), 8), 7:8]
    kinds = base_ref.shape[0]
    base = jnp.broadcast_to(base_ref[0:1, :], (8, 64))
    for s in range(1, kinds):
        base = jnp.where(spec == s, base_ref[s:s + 1, :], base)
    base_rows_ref[...] = jnp.concatenate([base] * 4, axis=0)
    for a in range(4):
        block = coupling_ref[0]
        for s in range(1, kinds):
            block = jnp.where(spec[a:a + 1, :] == s, coupling_ref[s], block)
        couple_ref[:, a * 64:(a + 1) * 64] = block
    w = occupations_ref[...] * (1.0 / (occupations_ref.shape[1] * bands))
    weights_ref[...] = jnp.concatenate([w, w], axis=1)


def own_tables(bands, own_row, grid, rhs, base, coupling, occupations):
    nrows = own_row.shape[0] * 4
    return pl.pallas_call(
        functools.partial(own_tables_kernel, bands),
        out_shape=(jax.ShapeDtypeStruct((nrows, rhs.shape[0]), BF16), jax.ShapeDtypeStruct((nrows, rhs.shape[1]), F32),
                   jax.ShapeDtypeStruct((64, 256), F32), jax.ShapeDtypeStruct((32, 64), F32),
                   jax.ShapeDtypeStruct((1, rhs.shape[1]), F32)),
        in_specs=[vmem()] * 4 + [hbm()] * 2,
        out_specs=(vmem(),) * 5,
        scratch_shapes=[pltpu.VMEM(coupling.shape, F32), pltpu.VMEM(occupations.shape, F32),
                        pltpu.SemaphoreType.DMA((2,))],
        compiler_params=LIMIT,
        name="own_tables",
    )(own_row, grid, rhs, base, in_hbm(coupling), in_hbm(occupations))


def occupancy_kernel(parts_ref, weights_ref, proj_ref, send_ref):
    total = parts_ref[0].astype(F32)
    for k in range(1, parts_ref.shape[0]):
        total = total + parts_ref[k].astype(F32)
    proj_ref[...] = total
    gram = dot_high(total * weights_ref[...], total, NT)
    gram = jnp.where(iota((32, 32), 0) % 4 == iota((32, 32), 1) % 4, gram, 0.0)
    lane = iota((32, 128), 1)
    spread = (iota((32, 128), 0) // 4 == lane % 8).astype(F32)
    wide = dot_high(gram, spread, NN)
    row = iota((32, 128), 0)
    wide = jnp.where(((lane // 8) % 8 == row // 4) & (lane // 64 == (row % 4) % 2), wide, 0.0)
    fold = ((iota((8, 32), 1) % 4) // 2 == iota((8, 32), 0)).astype(F32)
    flat = dot_high(fold, wide, NN)[0:2, :]
    for k in range(send_ref.shape[0]):
        send_ref[k] = flat


def occupancy_step(parts, weights, peers):
    _, nrows, width = parts.shape
    return pl.pallas_call(
        occupancy_kernel,
        out_shape=(jax.ShapeDtypeStruct((nrows, width), F32), jax.ShapeDtypeStruct((peers, 2, 128), F32)),
        in_specs=[vmem(), vmem()],
        out_specs=(vmem(), vmem()),
        compiler_params=LIMIT,
        name="occupancy",
    )(parts, weights)


def weigh_kernel(parts_ref, proj_ref, couple_ref, base_ref, onsite_ref, send_ref):
    occ = jnp.sum(parts_ref[...], axis=0)
    flat = jnp.concatenate([occ[0:1, :], occ[1:2, :]], axis=1)
    lane = iota((32, 256), 1)
    by_atom = jnp.where(lane // 64 == iota((32, 256), 0) % 4, flat, 0.0)
    onsite = dot_high(by_atom, couple_ref[...], NT) + base_ref[...]
    row = iota((32, 64), 0)
    onsite = jnp.where(iota((32, 64), 1) // 8 == row // 4, onsite, 0.0)
    spread = (iota((64, 32), 0) % 8 == iota((64, 32), 1) // 4).astype(F32)
    fold = (iota((64, 8), 0) % 8 == iota((64, 8), 1)).astype(F32)
    square = dot_high(onsite, fold, NN)
    for i in range(8):
        onsite_ref[:, i, :] = square[i * 4:i * 4 + 4, :]
    full = dot_high(onsite, spread, NN)
    full = jnp.where(iota((32, 32), 0) % 4 == iota((32, 32), 1) % 4, full, 0.0)
    weighted = dot_high(full, proj_ref[...], NN).astype(BF16)
    for k in range(send_ref.shape[0]):
        send_ref[k] = weighted


def weigh(parts, proj, couple, base_rows, peers):
    return pl.pallas_call(
        weigh_kernel,
        out_shape=(jax.ShapeDtypeStruct((4, 8, 8), F32), jax.ShapeDtypeStruct((peers, *proj.shape), BF16)),
        in_specs=[vmem()] * 4,
        out_specs=(vmem(), vmem()),
        compiler_params=LIMIT,
        name="weigh",
    )(parts, proj, couple, base_rows)


def product_with(table_ref, weighted_ref):
    width = weighted_ref.shape[1]
    gcount = table_ref.shape[1] // 2
    real, imag = weighted_ref[:, :width // 2], weighted_ref[:, width // 2:]
    turned = jnp.concatenate([-imag, real], axis=1)
    return (lax.dot_general(weighted_ref[...], table_ref[:, :gcount], TN, preferred_element_type=F32)
            + lax.dot_general(turned, table_ref[:, gcount:], TN, preferred_element_type=F32))


def back_kernel(table_ref, weighted_ref, out_ref):
    out_ref[...] = product_with(table_ref, weighted_ref)


def back_last_kernel(table_ref, weighted_ref, before_ref, out_ref):
    total = before_ref[...] + product_with(table_ref, weighted_ref)
    half = total.shape[0] // 2
    out_ref[0] = total[:half].T.astype(BF16)
    out_ref[1] = total[half:].T.astype(BF16)


def back_project(table, weighted, before=None):
    gcount, width = table.shape[1] // 2, weighted.shape[1]
    if before is None:
        return pl.pallas_call(
            back_kernel,
            out_shape=jax.ShapeDtypeStruct((width, gcount), F32),
            in_specs=[vmem()] * 2, out_specs=vmem(), compiler_params=LIMIT, name="back",
        )(table, weighted)
    return pl.pallas_call(
        back_last_kernel,
        out_shape=jax.ShapeDtypeStruct((2, gcount, width // 2), BF16),
        in_specs=[vmem()] * 3, out_specs=vmem(), compiler_params=LIMIT, name="back_last",
    )(table, weighted, before)


def local(wavefunctions, miller, reciprocal, fractional, species, atom_order, radial_widths,
          onsite_base, coupling, occupations):
    chips = lax.axis_size("chip")
    bands = lax.axis_size("band")
    swap = [(0, 1), (1, 0)]
    nb = wavefunctions.shape[2]
    other, other_proj, own_row, grid, rhs = other_tables(
        wavefunctions, miller, reciprocal, fractional, species, atom_order, radial_widths)
    received = lax.ppermute(other_proj, "core", swap)
    mine, mine_proj, couple, base_rows, weights = own_tables(
        bands, own_row, grid, rhs, onsite_base.reshape(-1, 64), coupling, occupations.reshape(1, -1))
    chip_sum = (mine_proj + received.astype(F32)).astype(BF16).reshape(chips, -1, 2 * nb)
    parts = lax.all_to_all(chip_sum, "chip", 0, 0, tiled=True)

    proj, occupancy = occupancy_step(parts, weights, bands)
    occupancy = lax.all_to_all(occupancy, "band", 0, 0, tiled=True)
    onsite, weighted = weigh(occupancy, proj, couple, base_rows, chips)
    weighted = lax.all_to_all(weighted, "chip", 0, 0, tiled=True).reshape(-1, 2 * nb)
    other_weighted = lax.ppermute(weighted, "core", swap)
    applied = back_project(mine, weighted)
    applied = back_project(other, other_weighted, applied)
    return applied, onsite


def solution(mesh):
    peers, bands = mesh.devices.shape
    inner = Mesh(mesh.devices.reshape(peers // 2, 2, bands), ("chip", "core", "band"))
    pw = ("chip", "core")
    placed = (P(None, pw, "band"), P(None, pw), P(), P(), P(), P(), P(), P(), P(), P("band"))
    return jax.shard_map(
        local,
        mesh=inner,
        in_specs=placed,
        out_specs=(P(None, pw, "band"), P(pw, None, None)),
        check_vma=False,
    )
```

```python
import functools
import math

import jax
import jax.numpy as jnp
from jax import lax
from jax.experimental import pallas as pl
from jax.experimental.pallas import tpu as pltpu
from jax.sharding import Mesh
from jax.sharding import PartitionSpec as P

HIGH = lax.Precision.HIGHEST
F32 = jnp.float32
BF16 = jnp.bfloat16
OTHER_ENDS = (8, 12, 16)
OWN_ENDS = (12, 16)
CHUNKS = 2
SIN = (6.283185005187988, -41.341590881347656, 81.59994506835938,
       -76.61447143554688, 41.3428840637207, -12.471243858337402)
COS = (1.0, -19.73920440673828, 64.93911743164062, -85.45014190673828,
       60.16762924194336, -25.967599868774414, 6.528658390045166)
NT = (((1,), (1,)), ((), ()))
TN = (((0,), (0,)), ((), ()))
NN = (((1,), (0,)), ((), ()))


LIMIT = pltpu.CompilerParams(vmem_limit_bytes=16 << 20)


def dot_high(left, right, dims):
    return lax.dot_general(left, right, dims, precision=HIGH, preferred_element_type=F32)


def iota(shape, dim):
    return lax.broadcasted_iota(jnp.int32, shape, dim)


def in_parts(array):
    high = array.astype(BF16).astype(F32)
    rest = array - high
    middle = rest.astype(BF16).astype(F32)
    return high, middle, rest - middle


def gather_lanes(array, order):
    rows, lanes = array.shape
    parts = jnp.concatenate(in_parts(array), axis=0).astype(BF16)
    chosen = (iota((lanes, lanes), 0) == order).astype(F32).astype(BF16)
    picked = jnp.dot(parts, chosen, preferred_element_type=F32)
    return picked[:rows] + picked[rows:2 * rows] + picked[2 * rows:]


def horner(coefficients, z):
    total = jnp.full_like(z, coefficients[-1])
    for c in coefficients[-2::-1]:
        total = total * z + c
    return total


def vmem():
    return pl.BlockSpec(memory_space=pltpu.VMEM)


def hbm():
    return pl.BlockSpec(memory_space=pltpu.HBM)


def in_hbm(array):
    return pltpu.with_memory_space_constraint(array, pltpu.HBM)


def fetch(pairs, copied):
    copies = [pltpu.make_async_copy(src, dst, copied.at[k]) for k, (src, dst) in enumerate(pairs)]
    for copy in copies:
        copy.start()
    return copies


def project_rows(by_row, grid_ref, rhs_ref, beta_ref, proj_ref, ends, before_first):
    done = 0
    gcount = grid_ref.shape[1]
    wide = (8, gcount)
    m, g = ([jnp.broadcast_to(grid_ref[d:d + 1, :], wide) for d in dims] for dims in ((0, 1, 2), (3, 4, 5)))
    g2 = jnp.broadcast_to(grid_ref[6:7, :], wide)
    first = iota(wide, 0) < 4
    pair_g = (None, jnp.where(first, g[0], g[1]), jnp.where(first, g[2], g[0]), jnp.where(first, g[1], g[2]))
    first1 = iota((8, 1), 0) < 4
    for q in range(by_row.shape[0] // 8):
        par = by_row[q * 8:q * 8 + 8, :]
        col = [par[:, k:k + 1] for k in range(7)]
        turns = col[0] * m[0] + col[1] * m[1] + col[2] * m[2]
        r = turns - jnp.round(turns)
        z = r * r
        sin = horner(SIN, z) * r
        cos = horner(COS, z)
        minus_sin = -sin
        pair_w = (jnp.where(first1, col[3], col[4]), col[5], jnp.where(first1, col[5], col[6]), col[6])
        re, im = [], []
        for p in range(4):
            w = pair_w[p]
            decay = jnp.exp(g2 * (-0.5 * (w * w)))
            if p == 0:
                re.append(decay * cos)
                im.append(decay * minus_sin)
            else:
                amp = pair_g[p] * ((-w) * decay)
                re.append(amp * sin)
                im.append(amp * cos)
        beta_ref[q * 32:q * 32 + 32, 0:gcount] = jnp.concatenate(re, axis=0).astype(BF16)
        beta_ref[q * 32:q * 32 + 32, gcount:] = jnp.concatenate(im, axis=0).astype(BF16)
        if q + 1 in ends:
            if done == 0:
                before_first()
            rows = slice(done * 32, (q + 1) * 32)
            proj_ref[rows, :] = jnp.dot(beta_ref[rows, :], rhs_ref[...],
                                        preferred_element_type=F32).astype(proj_ref.dtype)
            done = q + 1


def other_tables_kernel(recip_hbm, widths_hbm, wave_hbm, miller_hbm, frac_hbm, species_hbm, order_hbm,
                        beta_ref, proj_ref, own_row_ref, grid_ref, rhs_ref,
                        recip_ref, widths_ref, wave_ref, miller_ref, frac_ref, species_ref, order_ref, copied):
    loads = fetch(((wave_hbm, wave_ref), (recip_hbm, recip_ref), (widths_hbm, widths_ref), (miller_hbm, miller_ref),
                   (frac_hbm, frac_ref), (species_hbm, species_ref), (order_hbm, order_ref)), copied)
    for load in loads[1:]:
        load.wait()
    core = lax.axis_index("core")
    gcount = miller_ref.shape[1]
    natoms = order_ref.shape[1]
    owners = natoms // 8
    kinds = widths_ref.shape[0]
    spec = species_ref[...]
    rows = [frac_ref[d:d + 1, :] for d in range(3)]
    for c in range(4):
        row = jnp.zeros((1, natoms), F32)
        for s in range(kinds):
            row = jnp.where(spec == s, widths_ref[s:s + 1, c:c + 1], row)
        rows.append(row)
    rows.append(spec.astype(F32))
    by_slot = gather_lanes(jnp.concatenate(rows, axis=0), order_ref[...]).T
    low = iota((8, 8), 0) < 4
    first_four, last_four = [], []
    for q in range(owners):
        here = by_slot[q * 8:q * 8 + 8, :]
        turned = pltpu.roll(here, 4, 0)
        first_four.append(jnp.where(low, here, turned))
        last_four.append(jnp.where(low, turned, here))
    first_four = jnp.concatenate(first_four, axis=0)
    last_four = jnp.concatenate(last_four, axis=0)
    by_row = jnp.where(core == 0, last_four, first_four)
    own_row_ref[...] = jnp.where(core == 0, first_four, last_four)

    mil = miller_ref[...].astype(F32)
    m = [mil[d:d + 1, :] for d in range(3)]
    two_pi = 2.0 * math.pi
    g = [two_pi * (recip_ref[d:d + 1, 0:1] * m[0] + recip_ref[d:d + 1, 1:2] * m[1] + recip_ref[d:d + 1, 2:3] * m[2])
         for d in range(3)]
    g2 = g[0] * g[0] + g[1] * g[1] + g[2] * g[2]
    grid_ref[...] = jnp.concatenate([*m, *g, g2, g2], axis=0)

    def make_rhs():
        loads[0].wait()
        nb = wave_ref.shape[2]
        real, imag = wave_ref[0], wave_ref[1]
        rhs_ref[0:gcount, 0:nb] = real
        rhs_ref[0:gcount, nb:] = imag
        rhs_ref[gcount:, 0:nb] = imag
        rhs_ref[gcount:, nb:] = -real

    project_rows(by_row, grid_ref, rhs_ref, beta_ref, proj_ref, OTHER_ENDS, make_rhs)


def other_tables(wavefunctions, miller, reciprocal, fractional, species, atom_order, radial_widths):
    gcount, nb = wavefunctions.shape[1:]
    natoms = atom_order.shape[0]
    args = (reciprocal, radial_widths, wavefunctions, miller, fractional, species.reshape(1, -1),
            atom_order.reshape(1, -1))
    return pl.pallas_call(
        other_tables_kernel,
        out_shape=(jax.ShapeDtypeStruct((natoms * 4, 2 * gcount), BF16),
                   jax.ShapeDtypeStruct((natoms * 4, 2 * nb), BF16),
                   jax.ShapeDtypeStruct((natoms, 8), F32), jax.ShapeDtypeStruct((8, gcount), F32),
                   jax.ShapeDtypeStruct((2 * gcount, 2 * nb), BF16)),
        in_specs=[hbm()] * len(args),
        out_specs=(vmem(),) * 5,
        scratch_shapes=[pltpu.VMEM(a.shape, a.dtype) for a in args] + [pltpu.SemaphoreType.DMA((len(args),))],
        compiler_params=LIMIT,
        name="other_tables",
    )(*(in_hbm(a) for a in args))


def own_tables_kernel(bands, own_row_ref, grid_ref, rhs_ref, base_ref, coupling_hbm, occupations_hbm,
                      beta_ref, proj_ref, couple_ref, base_rows_ref, weights_ref,
                      coupling_ref, occupations_ref, copied):
    loads = fetch(((coupling_hbm, coupling_ref), (occupations_hbm, occupations_ref)), copied)
    chip = lax.axis_index("chip")

    def of_owned_atoms():
        for load in loads:
            load.wait()
        spec = own_row_ref[pl.ds(pl.multiple_of(chip * 8, 8), 8), 7:8]
        kinds = base_ref.shape[0]
        base = jnp.broadcast_to(base_ref[0:1, :], (8, 64))
        for s in range(1, kinds):
            base = jnp.where(spec == s, base_ref[s:s + 1, :], base)
        base_rows_ref[...] = base
        by_kind = [coupling_ref[s].T for s in range(kinds)]
        for a in range(4):
            for i in range(8):
                rows = slice(i * 8, i * 8 + 8)
                block = by_kind[0][rows]
                for s in range(1, kinds):
                    block = jnp.where(spec[a:a + 1, :] == s, by_kind[s][rows], block)
                to = ((i % 2) * 4 + i // 2) * 32 + a * 8
                couple_ref[to:to + 8, :] = block
        w = occupations_ref[...] * (1.0 / (occupations_ref.shape[1] * bands))
        weights_ref[...] = jnp.concatenate([w, w], axis=1)

    project_rows(own_row_ref[...], grid_ref, rhs_ref, beta_ref, proj_ref, OWN_ENDS, of_owned_atoms)


def own_tables(bands, own_row, grid, rhs, base, coupling, occupations):
    nrows = own_row.shape[0] * 4
    return pl.pallas_call(
        functools.partial(own_tables_kernel, bands),
        out_shape=(jax.ShapeDtypeStruct((nrows, rhs.shape[0]), BF16), jax.ShapeDtypeStruct((nrows, rhs.shape[1]), F32),
                   jax.ShapeDtypeStruct((256, 64), F32), jax.ShapeDtypeStruct((8, 64), F32),
                   jax.ShapeDtypeStruct((1, rhs.shape[1]), F32)),
        in_specs=[vmem()] * 4 + [hbm()] * 2,
        out_specs=(vmem(),) * 5,
        scratch_shapes=[pltpu.VMEM(coupling.shape, F32), pltpu.VMEM(occupations.shape, F32),
                        pltpu.SemaphoreType.DMA((2,))],
        compiler_params=LIMIT,
        name="own_tables",
    )(own_row, grid, rhs, base, in_hbm(coupling), in_hbm(occupations))


def occupancy_kernel(parts_ref, weights_ref, proj_ref, send_ref):
    total = parts_ref[0].astype(F32)
    for k in range(1, parts_ref.shape[0]):
        total = total + parts_ref[k].astype(F32)
    nb = proj_ref.shape[2]
    proj_ref[0] = total[:, :nb]
    proj_ref[1] = total[:, nb:]
    by_atom = jnp.concatenate([jnp.concatenate(
        [proj_ref[h, pl.ds(a, 8, stride=4), :] for a in range(4)], axis=0) for h in range(2)], axis=1)
    gram = dot_high(total * weights_ref[...], by_atom, NT)
    flat = jnp.concatenate([gram[k * 8:k * 8 + 8, :] for k in range(4)], axis=1)
    for k in range(send_ref.shape[0]):
        send_ref[k] = flat


def occupancy_step(parts, weights, peers):
    _, nrows, width = parts.shape
    return pl.pallas_call(
        occupancy_kernel,
        out_shape=(jax.ShapeDtypeStruct((2, nrows, width // 2), F32), jax.ShapeDtypeStruct((peers, 8, 128), F32)),
        in_specs=[vmem(), vmem()],
        out_specs=(vmem(), vmem()),
        compiler_params=LIMIT,
        name="occupancy",
    )(parts, weights)


def weigh_kernel(parts_ref, proj_ref, couple_ref, base_ref, onsite_ref, send_ref):
    occ = parts_ref[0]
    for k in range(1, parts_ref.shape[0]):
        occ = occ + parts_ref[k]
    row, lane = iota((8, 128), 0), iota((8, 128), 1)
    occ = jnp.where((lane // 8) % 4 == row % 4, occ, 0.0)
    by_parity = jnp.concatenate([jnp.where(row < 4, occ, 0.0), jnp.where(row < 4, 0.0, occ)], axis=1)
    response = dot_high(by_parity, couple_ref[...], NN)
    onsite = response + pltpu.roll(response, 4, 0) + base_ref[...]
    onsite_ref[...] = onsite
    pair = jnp.where(iota((8, 64), 0) < 4, onsite, jnp.concatenate([onsite[:, 8:], onsite[:, :8]], axis=1))
    low = iota((8, 2 * proj_ref.shape[2]), 0) < 4
    total = [None] * 4
    for k in range(4):
        here = jnp.concatenate([proj_ref[h, k * 8:k * 8 + 8, :] for h in range(2)], axis=1)
        turned = pltpu.roll(here, 4, 0)
        for j, both in ((2 * k, jnp.where(low, here, turned)), (2 * k + 1, jnp.where(low, turned, here))):
            for t in range(4):
                term = pair[:, 16 * t + j:16 * t + j + 1] * both
                total[t] = term if total[t] is None else total[t] + term
    weighted = jnp.concatenate(total, axis=0).astype(BF16)
    for k in range(send_ref.shape[0]):
        send_ref[k] = weighted


def weigh(parts, proj, couple, base_rows, peers):
    return pl.pallas_call(
        weigh_kernel,
        out_shape=(jax.ShapeDtypeStruct((8, 64), F32), jax.ShapeDtypeStruct((peers, proj.shape[1], 2 * proj.shape[2]), BF16)),
        in_specs=[vmem()] * 4,
        out_specs=(vmem(), vmem()),
        compiler_params=LIMIT,
        name="weigh",
    )(parts, proj, couple, base_rows)


def turned_by_i(weighted):
    half = weighted.shape[1] // 2
    return jnp.concatenate([-weighted[:, half:], weighted[:, :half]], axis=1)


def back_kernel(table_ref, weighted_ref, other_ref, onsite_ref, out_ref, other_t_ref, square_ref):
    for i in range(8):
        square_ref[:, i, :] = onsite_ref[0:4, i * 8:i * 8 + 8]
    gcount = table_ref.shape[1] // 2
    nrows = other_ref.shape[0]
    weighted = weighted_ref[...]
    total = (lax.dot_general(weighted, table_ref[:, :gcount], TN, preferred_element_type=F32)
             + lax.dot_general(turned_by_i(weighted), table_ref[:, gcount:], TN, preferred_element_type=F32))
    out_ref[...] = total.T
    other_t_ref[:, :nrows] = other_ref[:, :gcount].T
    other_t_ref[:, nrows:] = other_ref[:, gcount:].T


def back(table, weighted, other, onsite):
    gcount = table.shape[1] // 2
    return pl.pallas_call(
        back_kernel,
        out_shape=(jax.ShapeDtypeStruct((gcount, weighted.shape[1]), F32),
                   jax.ShapeDtypeStruct((gcount, 2 * other.shape[0]), BF16), jax.ShapeDtypeStruct((4, 8, 8), F32)),
        in_specs=[vmem()] * 4, out_specs=(vmem(),) * 3, compiler_params=LIMIT, name="back",
    )(table, weighted, other, onsite)


def back_last_kernel(table_ref, weighted_ref, before_ref, out_hbm, out_ref, copied):
    nrows, width = weighted_ref.shape
    half = width // 2
    weighted = weighted_ref[...]
    turned = turned_by_i(weighted)
    chunks = copied.shape[0]
    size = table_ref.shape[0] // chunks
    copies = []
    for k in range(chunks):
        rows = slice(k * size, (k + 1) * size)
        total = (before_ref[rows, :] + jnp.dot(table_ref[rows, :nrows], weighted, preferred_element_type=F32)
                 + jnp.dot(table_ref[rows, nrows:], turned, preferred_element_type=F32))
        out_ref[k, 0] = total[:, :half].astype(BF16)
        out_ref[k, 1] = total[:, half:].astype(BF16)
        copies.append(pltpu.make_async_copy(out_ref.at[k], out_hbm.at[:, pl.ds(k * size, size), :], copied.at[k]))
        copies[-1].start()
    for copy in copies:
        copy.wait()


def back_last(table, weighted, before):
    gcount, width = before.shape
    return pl.pallas_call(
        back_last_kernel,
        out_shape=jax.ShapeDtypeStruct((2, gcount, width // 2), BF16),
        in_specs=[vmem()] * 3, out_specs=hbm(),
        scratch_shapes=[pltpu.VMEM((CHUNKS, 2, gcount // CHUNKS, width // 2), BF16),
                        pltpu.SemaphoreType.DMA((CHUNKS,))],
        compiler_params=LIMIT, name="back_last",
    )(table, weighted, before)


def local(wavefunctions, miller, reciprocal, fractional, species, atom_order, radial_widths,
          onsite_base, coupling, occupations):
    chips = lax.axis_size("chip")
    bands = lax.axis_size("band")
    swap = [(0, 1), (1, 0)]
    nb = wavefunctions.shape[2]
    other, other_proj, own_row, grid, rhs = other_tables(
        wavefunctions, miller, reciprocal, fractional, species, atom_order, radial_widths)
    received = lax.ppermute(other_proj, "core", swap)
    mine, mine_proj, couple, base_rows, weights = own_tables(
        bands, own_row, grid, rhs, onsite_base.reshape(-1, 64), coupling, occupations.reshape(1, -1))
    chip_sum = (mine_proj + received.astype(F32)).astype(BF16).reshape(chips, -1, 2 * nb)
    parts = lax.all_to_all(chip_sum, "chip", 0, 0, tiled=True)

    proj, occupancy = occupancy_step(parts, weights, bands)
    occupancy = lax.all_to_all(occupancy, "band", 0, 0, tiled=True)
    onsite, weighted = weigh(occupancy, proj, couple, base_rows, chips)
    weighted = lax.all_to_all(weighted, "chip", 0, 0, tiled=True).reshape(-1, 2 * nb)
    other_weighted = lax.ppermute(weighted, "core", swap)
    before, other_t, onsite = back(mine, weighted, other, onsite)
    applied = back_last(other_t, other_weighted, before)
    return applied, onsite


def solution(mesh):
    peers, bands = mesh.devices.shape
    inner = Mesh(mesh.devices.reshape(peers // 2, 2, bands), ("chip", "core", "band"))
    pw = ("chip", "core")
    placed = (P(None, pw, "band"), P(None, pw), P(), P(), P(), P(), P(), P(), P(), P("band"))
    return jax.shard_map(
        local,
        mesh=inner,
        in_specs=placed,
        out_specs=(P(None, pw, "band"), P(pw, None, None)),
        check_vma=False,
    )
```

```python
import functools
import math

import jax
import jax.numpy as jnp
from jax import lax
from jax.experimental import pallas as pl
from jax.experimental.pallas import tpu as pltpu
from jax.sharding import Mesh
from jax.sharding import PartitionSpec as P

HIGH = lax.Precision.HIGHEST
F32 = jnp.float32
BF16 = jnp.bfloat16
OTHER_ENDS = (8, 14, 16)
OWN_ENDS = (12, 16)
CHUNKS = 4
SIN = (6.283185005187988, -41.341590881347656, 81.59994506835938,
       -76.61447143554688, 41.3428840637207, -12.471243858337402)
COS = (1.0, -19.73920440673828, 64.93911743164062, -85.45014190673828,
       60.16762924194336, -25.967599868774414, 6.528658390045166)
NT = (((1,), (1,)), ((), ()))
TN = (((0,), (0,)), ((), ()))
NN = (((1,), (0,)), ((), ()))


LIMIT = pltpu.CompilerParams(vmem_limit_bytes=16 << 20)


def dot_high(left, right, dims):
    return lax.dot_general(left, right, dims, precision=HIGH, preferred_element_type=F32)


def iota(shape, dim):
    return lax.broadcasted_iota(jnp.int32, shape, dim)


def in_parts(array):
    high = array.astype(BF16).astype(F32)
    rest = array - high
    middle = rest.astype(BF16).astype(F32)
    return high, middle, rest - middle


def gather_lanes(array, order):
    rows, lanes = array.shape
    parts = jnp.concatenate(in_parts(array), axis=0).astype(BF16)
    chosen = (iota((lanes, lanes), 0) == order).astype(F32).astype(BF16)
    picked = jnp.dot(parts, chosen, preferred_element_type=F32)
    return picked[:rows] + picked[rows:2 * rows] + picked[2 * rows:]


def horner(coefficients, z):
    total = jnp.full_like(z, coefficients[-1])
    for c in coefficients[-2::-1]:
        total = total * z + c
    return total


def vmem():
    return pl.BlockSpec(memory_space=pltpu.VMEM)


def hbm():
    return pl.BlockSpec(memory_space=pltpu.HBM)


def in_hbm(array):
    return pltpu.with_memory_space_constraint(array, pltpu.HBM)


def fetch(pairs, copied):
    copies = [pltpu.make_async_copy(src, dst, copied.at[k]) for k, (src, dst) in enumerate(pairs)]
    for copy in copies:
        copy.start()
    return copies


def project_rows(by_row, grid_ref, rhs_ref, beta_ref, proj_ref, ends, before_first):
    done = 0
    gcount = grid_ref.shape[1]
    wide = (8, gcount)
    m, g = ([jnp.broadcast_to(grid_ref[d:d + 1, :], wide) for d in dims] for dims in ((0, 1, 2), (3, 4, 5)))
    g2 = jnp.broadcast_to(grid_ref[6:7, :], wide)
    first = iota(wide, 0) < 4
    pair_g = (None, jnp.where(first, g[0], g[1]), jnp.where(first, g[2], g[0]), jnp.where(first, g[1], g[2]))
    first1 = iota((8, 1), 0) < 4
    for q in range(by_row.shape[0] // 8):
        par = by_row[q * 8:q * 8 + 8, :]
        col = [par[:, k:k + 1] for k in range(7)]
        turns = col[0] * m[0] + col[1] * m[1] + col[2] * m[2]
        r = turns - jnp.round(turns)
        z = r * r
        sin = horner(SIN, z) * r
        cos = horner(COS, z)
        minus_sin = -sin
        pair_w = (jnp.where(first1, col[3], col[4]), col[5], jnp.where(first1, col[5], col[6]), col[6])
        re, im = [], []
        for p in range(4):
            w = pair_w[p]
            decay = jnp.exp(g2 * (-0.5 * (w * w)))
            if p == 0:
                re.append(decay * cos)
                im.append(decay * minus_sin)
            else:
                amp = pair_g[p] * ((-w) * decay)
                re.append(amp * sin)
                im.append(amp * cos)
        beta_ref[q * 32:q * 32 + 32, 0:gcount] = jnp.concatenate(re, axis=0).astype(BF16)
        beta_ref[q * 32:q * 32 + 32, gcount:] = jnp.concatenate(im, axis=0).astype(BF16)
        if q + 1 in ends:
            if done == 0:
                before_first()
            rows = slice(done * 32, (q + 1) * 32)
            by_real = jnp.dot(beta_ref[rows, :gcount], rhs_ref[...], preferred_element_type=F32)
            by_imag = jnp.dot(beta_ref[rows, gcount:], rhs_ref[...], preferred_element_type=F32)
            half = rhs_ref.shape[1] // 2
            proj_ref[rows, :half] = (by_real[:, :half] + by_imag[:, half:]).astype(proj_ref.dtype)
            proj_ref[rows, half:] = (by_real[:, half:] - by_imag[:, :half]).astype(proj_ref.dtype)
            done = q + 1


def other_tables_kernel(recip_hbm, widths_hbm, wave_hbm, miller_hbm, frac_hbm, species_hbm, order_hbm,
                        beta_ref, proj_ref, own_row_ref, grid_ref, rhs_ref,
                        recip_ref, widths_ref, wave_ref, miller_ref, frac_ref, species_ref, order_ref, copied):
    loads = fetch(((wave_hbm, wave_ref), (recip_hbm, recip_ref), (widths_hbm, widths_ref), (miller_hbm, miller_ref),
                   (frac_hbm, frac_ref), (species_hbm, species_ref), (order_hbm, order_ref)), copied)
    for load in loads[1:]:
        load.wait()
    core = lax.axis_index("core")
    gcount = miller_ref.shape[1]
    natoms = order_ref.shape[1]
    owners = natoms // 8
    kinds = widths_ref.shape[0]
    spec = species_ref[...]
    rows = [frac_ref[d:d + 1, :] for d in range(3)]
    for c in range(4):
        row = jnp.zeros((1, natoms), F32)
        for s in range(kinds):
            row = jnp.where(spec == s, widths_ref[s:s + 1, c:c + 1], row)
        rows.append(row)
    rows.append(spec.astype(F32))
    by_slot = gather_lanes(jnp.concatenate(rows, axis=0), order_ref[...]).T
    low = iota((8, 8), 0) < 4
    first_four, last_four = [], []
    for q in range(owners):
        here = by_slot[q * 8:q * 8 + 8, :]
        turned = pltpu.roll(here, 4, 0)
        first_four.append(jnp.where(low, here, turned))
        last_four.append(jnp.where(low, turned, here))
    first_four = jnp.concatenate(first_four, axis=0)
    last_four = jnp.concatenate(last_four, axis=0)
    by_row = jnp.where(core == 0, last_four, first_four)
    own_row_ref[...] = jnp.where(core == 0, first_four, last_four)

    mil = miller_ref[...].astype(F32)
    m = [mil[d:d + 1, :] for d in range(3)]
    two_pi = 2.0 * math.pi
    g = [two_pi * (recip_ref[d:d + 1, 0:1] * m[0] + recip_ref[d:d + 1, 1:2] * m[1] + recip_ref[d:d + 1, 2:3] * m[2])
         for d in range(3)]
    g2 = g[0] * g[0] + g[1] * g[1] + g[2] * g[2]
    grid_ref[...] = jnp.concatenate([*m, *g, g2, g2], axis=0)

    def make_rhs():
        loads[0].wait()
        nb = wave_ref.shape[2]
        rhs_ref[:, :nb] = wave_ref[0]
        rhs_ref[:, nb:] = wave_ref[1]

    project_rows(by_row, grid_ref, rhs_ref, beta_ref, proj_ref, OTHER_ENDS, make_rhs)


def other_tables(wavefunctions, miller, reciprocal, fractional, species, atom_order, radial_widths):
    gcount, nb = wavefunctions.shape[1:]
    natoms = atom_order.shape[0]
    args = (reciprocal, radial_widths, wavefunctions, miller, fractional, species.reshape(1, -1),
            atom_order.reshape(1, -1))
    return pl.pallas_call(
        other_tables_kernel,
        out_shape=(jax.ShapeDtypeStruct((natoms * 4, 2 * gcount), BF16),
                   jax.ShapeDtypeStruct((natoms * 4, 2 * nb), BF16),
                   jax.ShapeDtypeStruct((natoms, 8), F32), jax.ShapeDtypeStruct((8, gcount), F32),
                   jax.ShapeDtypeStruct((gcount, 2 * nb), BF16)),
        in_specs=[hbm()] * len(args),
        out_specs=(vmem(),) * 5,
        scratch_shapes=[pltpu.VMEM(a.shape, a.dtype) for a in args] + [pltpu.SemaphoreType.DMA((len(args),))],
        compiler_params=LIMIT,
        name="other_tables",
    )(*(in_hbm(a) for a in args))


def own_tables_kernel(bands, own_row_ref, grid_ref, rhs_ref, base_ref, coupling_hbm, occupations_hbm,
                      beta_ref, proj_ref, couple_ref, base_rows_ref, weights_ref,
                      coupling_ref, occupations_ref, copied):
    loads = fetch(((coupling_hbm, coupling_ref), (occupations_hbm, occupations_ref)), copied)
    chip = lax.axis_index("chip")

    def of_owned_atoms():
        for load in loads:
            load.wait()
        spec = own_row_ref[pl.ds(pl.multiple_of(chip * 8, 8), 8), 7:8]
        kinds = base_ref.shape[0]
        base = jnp.broadcast_to(base_ref[0:1, :], (8, 64))
        for s in range(1, kinds):
            base = jnp.where(spec == s, base_ref[s:s + 1, :], base)
        base_rows_ref[...] = base
        by_kind = [coupling_ref[s].T for s in range(kinds)]
        for a in range(4):
            for i in range(8):
                rows = slice(i * 8, i * 8 + 8)
                block = by_kind[0][rows]
                for s in range(1, kinds):
                    block = jnp.where(spec[a:a + 1, :] == s, by_kind[s][rows], block)
                to = ((i % 2) * 4 + i // 2) * 32 + a * 8
                couple_ref[to:to + 8, :] = block
        w = occupations_ref[...] * (1.0 / (occupations_ref.shape[1] * bands))
        weights_ref[...] = jnp.concatenate([w, w], axis=1)

    project_rows(own_row_ref[...], grid_ref, rhs_ref, beta_ref, proj_ref, OWN_ENDS, of_owned_atoms)


def own_tables(bands, own_row, grid, rhs, base, coupling, occupations):
    nrows = own_row.shape[0] * 4
    return pl.pallas_call(
        functools.partial(own_tables_kernel, bands),
        out_shape=(jax.ShapeDtypeStruct((nrows, 2 * rhs.shape[0]), BF16), jax.ShapeDtypeStruct((nrows, rhs.shape[1]), F32),
                   jax.ShapeDtypeStruct((256, 64), F32), jax.ShapeDtypeStruct((8, 64), F32),
                   jax.ShapeDtypeStruct((1, rhs.shape[1]), F32)),
        in_specs=[vmem()] * 4 + [hbm()] * 2,
        out_specs=(vmem(),) * 5,
        scratch_shapes=[pltpu.VMEM(coupling.shape, F32), pltpu.VMEM(occupations.shape, F32),
                        pltpu.SemaphoreType.DMA((2,))],
        compiler_params=LIMIT,
        name="own_tables",
    )(own_row, grid, rhs, base, in_hbm(coupling), in_hbm(occupations))


def occupancy_kernel(parts_ref, weights_ref, proj_ref, send_ref):
    total = parts_ref[0].astype(F32)
    for k in range(1, parts_ref.shape[0]):
        total = total + parts_ref[k].astype(F32)
    nb = proj_ref.shape[2]
    proj_ref[0] = total[:, :nb]
    proj_ref[1] = total[:, nb:]
    by_atom = jnp.concatenate([jnp.concatenate(
        [proj_ref[h, pl.ds(a, 8, stride=4), :] for a in range(4)], axis=0) for h in range(2)], axis=1)
    gram = dot_high(total * weights_ref[...], by_atom, NT)
    flat = jnp.concatenate([gram[k * 8:k * 8 + 8, :] for k in range(4)], axis=1)
    flat = jnp.where((iota((8, 128), 1) // 8) % 4 == iota((8, 128), 0) % 4, flat, 0.0)
    flat = flat + pltpu.roll(flat, 1, 0)
    flat = flat + pltpu.roll(flat, 2, 0)
    flat = jnp.concatenate([flat[3:4, :], flat[7:8, :]], axis=0)
    for k in range(send_ref.shape[0]):
        send_ref[k] = flat


def occupancy_step(parts, weights, peers):
    _, nrows, width = parts.shape
    return pl.pallas_call(
        occupancy_kernel,
        out_shape=(jax.ShapeDtypeStruct((2, nrows, width // 2), F32), jax.ShapeDtypeStruct((peers, 2, 128), F32)),
        in_specs=[vmem(), vmem()],
        out_specs=(vmem(), vmem()),
        compiler_params=LIMIT,
        name="occupancy",
    )(parts, weights)


def weigh_kernel(parts_ref, proj_ref, couple_ref, base_ref, onsite_ref, send_ref):
    occ = parts_ref[0]
    for k in range(1, parts_ref.shape[0]):
        occ = occ + parts_ref[k]
    occ = jnp.concatenate([occ[0:1, :], occ[1:2, :]], axis=1)
    own_atom = (iota((8, 256), 1) // 8) % 4 == iota((8, 256), 0) % 4
    onsite = dot_high(jnp.where(own_atom, occ, 0.0), couple_ref[...], NN) + base_ref[...]
    onsite_ref[...] = onsite
    pair = jnp.where(iota((8, 64), 0) < 4, onsite, jnp.concatenate([onsite[:, 8:], onsite[:, :8]], axis=1))
    low = iota((8, 2 * proj_ref.shape[2]), 0) < 4
    total = [None] * 4
    for k in range(4):
        here = jnp.concatenate([proj_ref[h, k * 8:k * 8 + 8, :] for h in range(2)], axis=1)
        turned = pltpu.roll(here, 4, 0)
        for j, both in ((2 * k, jnp.where(low, here, turned)), (2 * k + 1, jnp.where(low, turned, here))):
            for t in range(4):
                term = pair[:, 16 * t + j:16 * t + j + 1] * both
                total[t] = term if total[t] is None else total[t] + term
    weighted = jnp.concatenate(total, axis=0).astype(BF16)
    for k in range(send_ref.shape[0]):
        send_ref[k] = weighted


def weigh(parts, proj, couple, base_rows, peers):
    return pl.pallas_call(
        weigh_kernel,
        out_shape=(jax.ShapeDtypeStruct((8, 64), F32), jax.ShapeDtypeStruct((peers, proj.shape[1], 2 * proj.shape[2]), BF16)),
        in_specs=[vmem()] * 4,
        out_specs=(vmem(), vmem()),
        compiler_params=LIMIT,
        name="weigh",
    )(parts, proj, couple, base_rows)


def turned_by_i(weighted):
    half = weighted.shape[1] // 2
    return jnp.concatenate([-weighted[:, half:], weighted[:, :half]], axis=1)


def back_kernel(table_ref, weighted_ref, other_ref, onsite_ref, out_ref, other_t_ref, square_ref):
    for i in range(8):
        square_ref[:, i, :] = onsite_ref[0:4, i * 8:i * 8 + 8]
    gcount = table_ref.shape[1] // 2
    weighted = weighted_ref[...]
    total = (lax.dot_general(weighted, table_ref[:, :gcount], TN, preferred_element_type=F32)
             + lax.dot_general(turned_by_i(weighted), table_ref[:, gcount:], TN, preferred_element_type=F32))
    out_ref[...] = total.T
    other_t_ref[0] = other_ref[:, :gcount].T
    other_t_ref[1] = other_ref[:, gcount:].T


def back(table, weighted, other, onsite):
    gcount = table.shape[1] // 2
    return pl.pallas_call(
        back_kernel,
        out_shape=(jax.ShapeDtypeStruct((gcount, weighted.shape[1]), F32),
                   jax.ShapeDtypeStruct((2, gcount, other.shape[0]), BF16), jax.ShapeDtypeStruct((4, 8, 8), F32)),
        in_specs=[vmem()] * 4, out_specs=(vmem(),) * 3, compiler_params=LIMIT, name="back",
    )(table, weighted, other, onsite)


def back_last_kernel(table_ref, weighted_ref, before_ref, out_hbm, out_ref, copied):
    half = weighted_ref.shape[1] // 2
    weighted = weighted_ref[...]
    chunks = copied.shape[0]
    size = table_ref.shape[1] // chunks
    copies = []
    for k in range(chunks):
        rows = slice(k * size, (k + 1) * size)
        by_real = jnp.dot(table_ref[0, rows, :], weighted, preferred_element_type=F32)
        by_imag = jnp.dot(table_ref[1, rows, :], weighted, preferred_element_type=F32)
        out_ref[k, 0] = (before_ref[rows, :half] + (by_real[:, :half] - by_imag[:, half:])).astype(BF16)
        out_ref[k, 1] = (before_ref[rows, half:] + (by_real[:, half:] + by_imag[:, :half])).astype(BF16)
        copies.append(pltpu.make_async_copy(out_ref.at[k], out_hbm.at[:, pl.ds(k * size, size), :], copied.at[k]))
        copies[-1].start()
    for copy in copies:
        copy.wait()


def back_last(table, weighted, before):
    gcount, width = before.shape
    return pl.pallas_call(
        back_last_kernel,
        out_shape=jax.ShapeDtypeStruct((2, gcount, width // 2), BF16),
        in_specs=[vmem()] * 3, out_specs=hbm(),
        scratch_shapes=[pltpu.VMEM((CHUNKS, 2, gcount // CHUNKS, width // 2), BF16),
                        pltpu.SemaphoreType.DMA((CHUNKS,))],
        compiler_params=LIMIT, name="back_last",
    )(table, weighted, before)


def local(wavefunctions, miller, reciprocal, fractional, species, atom_order, radial_widths,
          onsite_base, coupling, occupations):
    chips = lax.axis_size("chip")
    bands = lax.axis_size("band")
    swap = [(0, 1), (1, 0)]
    nb = wavefunctions.shape[2]
    other, other_proj, own_row, grid, rhs = other_tables(
        wavefunctions, miller, reciprocal, fractional, species, atom_order, radial_widths)
    received = lax.ppermute(other_proj, "core", swap)
    mine, mine_proj, couple, base_rows, weights = own_tables(
        bands, own_row, grid, rhs, onsite_base.reshape(-1, 64), coupling, occupations.reshape(1, -1))
    chip_sum = (mine_proj + received.astype(F32)).astype(BF16).reshape(chips, -1, 2 * nb)
    parts = lax.all_to_all(chip_sum, "chip", 0, 0, tiled=True)

    proj, occupancy = occupancy_step(parts, weights, bands)
    occupancy = lax.all_to_all(occupancy, "band", 0, 0, tiled=True)
    onsite, weighted = weigh(occupancy, proj, couple, base_rows, chips)
    weighted = lax.all_to_all(weighted, "chip", 0, 0, tiled=True).reshape(-1, 2 * nb)
    other_weighted = lax.ppermute(weighted, "core", swap)
    before, other_t, onsite = back(mine, weighted, other, onsite)
    applied = back_last(other_t, other_weighted, before)
    return applied, onsite


def solution(mesh):
    peers, bands = mesh.devices.shape
    inner = Mesh(mesh.devices.reshape(peers // 2, 2, bands), ("chip", "core", "band"))
    pw = ("chip", "core")
    placed = (P(None, pw, "band"), P(None, pw), P(), P(), P(), P(), P(), P(), P(), P("band"))
    return jax.shard_map(
        local,
        mesh=inner,
        in_specs=placed,
        out_specs=(P(None, pw, "band"), P(pw, None, None)),
        check_vma=False,
    )
```

```python
import functools
import math

import jax
import jax.numpy as jnp
from jax import lax
from jax.experimental import pallas as pl
from jax.experimental.pallas import tpu as pltpu
from jax.sharding import Mesh
from jax.sharding import PartitionSpec as P

HIGH = lax.Precision.HIGHEST
F32 = jnp.float32
BF16 = jnp.bfloat16
OTHER_ENDS = (8, 14, 16)
OWN_ENDS = (12, 16)
CHUNKS = 4
SIN = (6.283185005187988, -41.341590881347656, 81.59994506835938,
       -76.61447143554688, 41.3428840637207, -12.471243858337402)
COS = (1.0, -19.73920440673828, 64.93911743164062, -85.45014190673828,
       60.16762924194336, -25.967599868774414, 6.528658390045166)
NT = (((1,), (1,)), ((), ()))
TN = (((0,), (0,)), ((), ()))
NN = (((1,), (0,)), ((), ()))


LIMIT = pltpu.CompilerParams(vmem_limit_bytes=16 << 20)


def dot_high(left, right, dims):
    return lax.dot_general(left, right, dims, precision=HIGH, preferred_element_type=F32)


def iota(shape, dim):
    return lax.broadcasted_iota(jnp.int32, shape, dim)


def in_parts(array):
    high = array.astype(BF16).astype(F32)
    rest = array - high
    middle = rest.astype(BF16).astype(F32)
    return high, middle, rest - middle


def gather_lanes(array, order):
    rows, lanes = array.shape
    parts = jnp.concatenate(in_parts(array), axis=0).astype(BF16)
    chosen = (iota((lanes, lanes), 0) == order).astype(F32).astype(BF16)
    picked = jnp.dot(parts, chosen, preferred_element_type=F32)
    return picked[:rows] + picked[rows:2 * rows] + picked[2 * rows:]


def horner(coefficients, z):
    total = jnp.full_like(z, coefficients[-1])
    for c in coefficients[-2::-1]:
        total = total * z + c
    return total


def vmem():
    return pl.BlockSpec(memory_space=pltpu.VMEM)


def hbm():
    return pl.BlockSpec(memory_space=pltpu.HBM)


def in_hbm(array):
    return pltpu.with_memory_space_constraint(array, pltpu.HBM)


def fetch(pairs, copied):
    copies = [pltpu.make_async_copy(src, dst, copied.at[k]) for k, (src, dst) in enumerate(pairs)]
    for copy in copies:
        copy.start()
    return copies


def project_rows(owners, by_row, grid_ref, rhs_ref, beta_ref, proj_ref, ends, before_first):
    done = 0
    gcount = grid_ref.shape[1]
    wide = (8, gcount)
    m, g = ([jnp.broadcast_to(grid_ref[d:d + 1, :], wide) for d in dims] for dims in ((0, 1, 2), (3, 4, 5)))
    g2 = jnp.broadcast_to(grid_ref[6:7, :], wide)
    first = iota(wide, 0) < 4
    pair_g = (None, jnp.where(first, g[0], g[1]), jnp.where(first, g[2], g[0]), jnp.where(first, g[1], g[2]))
    first1 = iota((8, 1), 0) < 4
    for q, chip in enumerate(owners):
        par = by_row[chip * 8:chip * 8 + 8, :]
        col = [par[:, k:k + 1] for k in range(7)]
        turns = col[0] * m[0] + col[1] * m[1] + col[2] * m[2]
        r = turns - jnp.round(turns)
        z = r * r
        sin = horner(SIN, z) * r
        cos = horner(COS, z)
        minus_sin = -sin
        pair_w = (jnp.where(first1, col[3], col[4]), col[5], jnp.where(first1, col[5], col[6]), col[6])
        re, im = [], []
        for p in range(4):
            w = pair_w[p]
            decay = jnp.exp(g2 * (-0.5 * (w * w)))
            if p == 0:
                re.append(decay * cos)
                im.append(decay * minus_sin)
            else:
                amp = pair_g[p] * ((-w) * decay)
                re.append(amp * sin)
                im.append(amp * cos)
        beta_ref[q * 32:q * 32 + 32, 0:gcount] = jnp.concatenate(re, axis=0).astype(BF16)
        beta_ref[q * 32:q * 32 + 32, gcount:] = jnp.concatenate(im, axis=0).astype(BF16)
        if q + 1 in ends:
            if done == 0:
                before_first()
            rows = slice(done * 32, (q + 1) * 32)
            by_real = jnp.dot(beta_ref[rows, :gcount], rhs_ref[...], preferred_element_type=F32)
            by_imag = jnp.dot(beta_ref[rows, gcount:], rhs_ref[...], preferred_element_type=F32)
            half = rhs_ref.shape[1] // 2
            proj_ref[rows, :half] = (by_real[:, :half] + by_imag[:, half:]).astype(proj_ref.dtype)
            proj_ref[rows, half:] = (by_real[:, half:] - by_imag[:, :half]).astype(proj_ref.dtype)
            done = q + 1


def other_tables_kernel(owners, recip_hbm, widths_hbm, wave_hbm, miller_hbm, frac_hbm, species_hbm, order_hbm,
                        beta_ref, proj_ref, own_row_ref, grid_ref, rhs_ref,
                        recip_ref, widths_ref, wave_ref, miller_ref, frac_ref, species_ref, order_ref, copied):
    loads = fetch(((wave_hbm, wave_ref), (recip_hbm, recip_ref), (widths_hbm, widths_ref), (miller_hbm, miller_ref),
                   (frac_hbm, frac_ref), (species_hbm, species_ref), (order_hbm, order_ref)), copied)
    for load in loads[1:]:
        load.wait()
    core = lax.axis_index("core")
    gcount = miller_ref.shape[1]
    natoms = order_ref.shape[1]
    kinds = widths_ref.shape[0]
    spec = species_ref[...]
    rows = [frac_ref[d:d + 1, :] for d in range(3)]
    for c in range(4):
        row = jnp.zeros((1, natoms), F32)
        for s in range(kinds):
            row = jnp.where(spec == s, widths_ref[s:s + 1, c:c + 1], row)
        rows.append(row)
    rows.append(spec.astype(F32))
    by_slot = gather_lanes(jnp.concatenate(rows, axis=0), order_ref[...]).T
    low = iota((8, 8), 0) < 4
    first_four, last_four = [], []
    for q in range(len(owners)):
        here = by_slot[q * 8:q * 8 + 8, :]
        turned = pltpu.roll(here, 4, 0)
        first_four.append(jnp.where(low, here, turned))
        last_four.append(jnp.where(low, turned, here))
    first_four = jnp.concatenate(first_four, axis=0)
    last_four = jnp.concatenate(last_four, axis=0)
    by_row = jnp.where(core == 0, last_four, first_four)
    own_row_ref[...] = jnp.where(core == 0, first_four, last_four)

    mil = miller_ref[...].astype(F32)
    m = [mil[d:d + 1, :] for d in range(3)]
    two_pi = 2.0 * math.pi
    g = [two_pi * (recip_ref[d:d + 1, 0:1] * m[0] + recip_ref[d:d + 1, 1:2] * m[1] + recip_ref[d:d + 1, 2:3] * m[2])
         for d in range(3)]
    g2 = g[0] * g[0] + g[1] * g[1] + g[2] * g[2]
    grid_ref[...] = jnp.concatenate([*m, *g, g2, g2], axis=0)

    def make_rhs():
        loads[0].wait()
        nb = wave_ref.shape[2]
        rhs_ref[:, :nb] = wave_ref[0]
        rhs_ref[:, nb:] = wave_ref[1]

    project_rows(owners, by_row, grid_ref, rhs_ref, beta_ref, proj_ref, OTHER_ENDS, make_rhs)


def other_tables(owners, wavefunctions, miller, reciprocal, fractional, species, atom_order, radial_widths):
    gcount, nb = wavefunctions.shape[1:]
    natoms = atom_order.shape[0]
    args = (reciprocal, radial_widths, wavefunctions, miller, fractional, species.reshape(1, -1),
            atom_order.reshape(1, -1))
    return pl.pallas_call(
        functools.partial(other_tables_kernel, owners),
        out_shape=(jax.ShapeDtypeStruct((natoms * 4, 2 * gcount), BF16),
                   jax.ShapeDtypeStruct((natoms * 4, 2 * nb), BF16),
                   jax.ShapeDtypeStruct((natoms, 8), F32), jax.ShapeDtypeStruct((8, gcount), F32),
                   jax.ShapeDtypeStruct((gcount, 2 * nb), BF16)),
        in_specs=[hbm()] * len(args),
        out_specs=(vmem(),) * 5,
        scratch_shapes=[pltpu.VMEM(a.shape, a.dtype) for a in args] + [pltpu.SemaphoreType.DMA((len(args),))],
        compiler_params=LIMIT,
        name="other_tables",
    )(*(in_hbm(a) for a in args))


def own_tables_kernel(bands, owners, own_row_ref, grid_ref, rhs_ref, base_ref, coupling_hbm, occupations_hbm,
                      beta_ref, proj_ref, couple_ref, base_rows_ref, weights_ref,
                      coupling_ref, occupations_ref, copied):
    loads = fetch(((coupling_hbm, coupling_ref), (occupations_hbm, occupations_ref)), copied)
    chip = lax.axis_index("chip")

    def of_owned_atoms():
        for load in loads:
            load.wait()
        spec = own_row_ref[pl.ds(pl.multiple_of(chip * 8, 8), 8), 7:8]
        kinds = base_ref.shape[0]
        base = jnp.broadcast_to(base_ref[0:1, :], (8, 64))
        for s in range(1, kinds):
            base = jnp.where(spec == s, base_ref[s:s + 1, :], base)
        base_rows_ref[...] = base
        by_kind = [coupling_ref[s].T for s in range(kinds)]
        for a in range(4):
            for i in range(8):
                rows = slice(i * 8, i * 8 + 8)
                block = by_kind[0][rows]
                for s in range(1, kinds):
                    block = jnp.where(spec[a:a + 1, :] == s, by_kind[s][rows], block)
                to = ((i % 2) * 4 + i // 2) * 32 + a * 8
                couple_ref[to:to + 8, :] = block
        w = occupations_ref[...] * (1.0 / (occupations_ref.shape[1] * bands))
        weights_ref[...] = jnp.concatenate([w, w], axis=1)

    project_rows(owners, own_row_ref[...], grid_ref, rhs_ref, beta_ref, proj_ref, OWN_ENDS, of_owned_atoms)


def own_tables(bands, owners, own_row, grid, rhs, base, coupling, occupations):
    nrows = own_row.shape[0] * 4
    return pl.pallas_call(
        functools.partial(own_tables_kernel, bands, owners),
        out_shape=(jax.ShapeDtypeStruct((nrows, 2 * rhs.shape[0]), BF16), jax.ShapeDtypeStruct((nrows, rhs.shape[1]), F32),
                   jax.ShapeDtypeStruct((256, 64), F32), jax.ShapeDtypeStruct((8, 64), F32),
                   jax.ShapeDtypeStruct((1, rhs.shape[1]), F32)),
        in_specs=[vmem()] * 4 + [hbm()] * 2,
        out_specs=(vmem(),) * 5,
        scratch_shapes=[pltpu.VMEM(coupling.shape, F32), pltpu.VMEM(occupations.shape, F32),
                        pltpu.SemaphoreType.DMA((2,))],
        compiler_params=LIMIT,
        name="own_tables",
    )(own_row, grid, rhs, base, in_hbm(coupling), in_hbm(occupations))


def occupancy_kernel(parts_ref, weights_ref, proj_ref, send_ref):
    total = parts_ref[0].astype(F32)
    for k in range(1, parts_ref.shape[0]):
        total = total + parts_ref[k].astype(F32)
    nb = proj_ref.shape[2]
    proj_ref[0] = total[:, :nb]
    proj_ref[1] = total[:, nb:]
    by_atom = jnp.concatenate([jnp.concatenate(
        [proj_ref[h, pl.ds(a, 8, stride=4), :] for a in range(4)], axis=0) for h in range(2)], axis=1)
    gram = dot_high(total * weights_ref[...], by_atom, NT)
    flat = jnp.concatenate([gram[k * 8:k * 8 + 8, :] for k in range(4)], axis=1)
    flat = jnp.where((iota((8, 128), 1) // 8) % 4 == iota((8, 128), 0) % 4, flat, 0.0)
    flat = flat + pltpu.roll(flat, 1, 0)
    flat = flat + pltpu.roll(flat, 2, 0)
    flat = jnp.concatenate([flat[3:4, :], flat[7:8, :]], axis=0)
    for k in range(send_ref.shape[0]):
        send_ref[k] = flat


def occupancy_step(parts, weights, peers):
    _, nrows, width = parts.shape
    return pl.pallas_call(
        occupancy_kernel,
        out_shape=(jax.ShapeDtypeStruct((2, nrows, width // 2), F32), jax.ShapeDtypeStruct((peers, 2, 128), F32)),
        in_specs=[vmem(), vmem()],
        out_specs=(vmem(), vmem()),
        compiler_params=LIMIT,
        name="occupancy",
    )(parts, weights)


def weigh_kernel(parts_ref, proj_ref, couple_ref, base_ref, onsite_ref, send_ref):
    occ = parts_ref[0]
    for k in range(1, parts_ref.shape[0]):
        occ = occ + parts_ref[k]
    occ = jnp.concatenate([occ[0:1, :], occ[1:2, :]], axis=1)
    own_atom = (iota((8, 256), 1) // 8) % 4 == iota((8, 256), 0) % 4
    onsite = dot_high(jnp.where(own_atom, occ, 0.0), couple_ref[...], NN) + base_ref[...]
    onsite_ref[...] = onsite
    pair = jnp.where(iota((8, 64), 0) < 4, onsite, jnp.concatenate([onsite[:, 8:], onsite[:, :8]], axis=1))
    low = iota((8, 2 * proj_ref.shape[2]), 0) < 4
    total = [None] * 4
    for k in range(4):
        here = jnp.concatenate([proj_ref[h, k * 8:k * 8 + 8, :] for h in range(2)], axis=1)
        turned = pltpu.roll(here, 4, 0)
        for j, both in ((2 * k, jnp.where(low, here, turned)), (2 * k + 1, jnp.where(low, turned, here))):
            for t in range(4):
                term = pair[:, 16 * t + j:16 * t + j + 1] * both
                total[t] = term if total[t] is None else total[t] + term
    weighted = jnp.concatenate(total, axis=0).astype(BF16)
    for k in range(send_ref.shape[0]):
        send_ref[k] = weighted


def weigh(parts, proj, couple, base_rows, peers):
    return pl.pallas_call(
        weigh_kernel,
        out_shape=(jax.ShapeDtypeStruct((8, 64), F32), jax.ShapeDtypeStruct((peers, proj.shape[1], 2 * proj.shape[2]), BF16)),
        in_specs=[vmem()] * 4,
        out_specs=(vmem(), vmem()),
        compiler_params=LIMIT,
        name="weigh",
    )(parts, proj, couple, base_rows)


def turned_by_i(weighted):
    half = weighted.shape[1] // 2
    return jnp.concatenate([-weighted[:, half:], weighted[:, :half]], axis=1)


def back_kernel(table_ref, weighted_ref, other_ref, onsite_ref, out_ref, other_t_ref, square_ref):
    for i in range(8):
        square_ref[:, i, :] = onsite_ref[0:4, i * 8:i * 8 + 8]
    gcount = table_ref.shape[1] // 2
    weighted = weighted_ref[...]
    total = (lax.dot_general(weighted, table_ref[:, :gcount], TN, preferred_element_type=F32)
             + lax.dot_general(turned_by_i(weighted), table_ref[:, gcount:], TN, preferred_element_type=F32))
    out_ref[...] = total.T
    other_t_ref[0] = other_ref[:, :gcount].T
    other_t_ref[1] = other_ref[:, gcount:].T


def back(table, weighted, other, onsite):
    gcount = table.shape[1] // 2
    return pl.pallas_call(
        back_kernel,
        out_shape=(jax.ShapeDtypeStruct((gcount, weighted.shape[1]), F32),
                   jax.ShapeDtypeStruct((2, gcount, other.shape[0]), BF16), jax.ShapeDtypeStruct((4, 8, 8), F32)),
        in_specs=[vmem()] * 4, out_specs=(vmem(),) * 3, compiler_params=LIMIT, name="back",
    )(table, weighted, other, onsite)


def back_last_kernel(table_ref, weighted_ref, before_ref, out_hbm, out_ref, copied):
    half = weighted_ref.shape[1] // 2
    weighted = weighted_ref[...]
    chunks = copied.shape[0]
    size = table_ref.shape[1] // chunks
    copies = []
    for k in range(chunks):
        rows = slice(k * size, (k + 1) * size)
        by_real = jnp.dot(table_ref[0, rows, :], weighted, preferred_element_type=F32)
        by_imag = jnp.dot(table_ref[1, rows, :], weighted, preferred_element_type=F32)
        out_ref[k, 0] = (before_ref[rows, :half] + (by_real[:, :half] - by_imag[:, half:])).astype(BF16)
        out_ref[k, 1] = (before_ref[rows, half:] + (by_real[:, half:] + by_imag[:, :half])).astype(BF16)
        copies.append(pltpu.make_async_copy(out_ref.at[k], out_hbm.at[:, pl.ds(k * size, size), :], copied.at[k]))
        copies[-1].start()
    for copy in copies:
        copy.wait()


def back_last(table, weighted, before):
    gcount, width = before.shape
    return pl.pallas_call(
        back_last_kernel,
        out_shape=jax.ShapeDtypeStruct((2, gcount, width // 2), BF16),
        in_specs=[vmem()] * 3, out_specs=hbm(),
        scratch_shapes=[pltpu.VMEM((CHUNKS, 2, gcount // CHUNKS, width // 2), BF16),
                        pltpu.SemaphoreType.DMA((CHUNKS,))],
        compiler_params=LIMIT, name="back_last",
    )(table, weighted, before)


def farthest_first(places, extents, first):
    def distance(i):
        steps = [abs(a - b) for a, b in zip(places[i], places[first])]
        return sum(min(s, n - s) for s, n in zip(steps, extents))
    others = [i for i in range(len(places)) if i != first]
    return [first] + sorted(others, key=lambda i: (-distance(i), (i - first) % len(places)))


def exchange(blocks, axis, members):
    return lax.all_to_all(blocks, axis, 0, 0, axis_index_groups=[members], tiled=True)


def local(wavefunctions, miller, reciprocal, fractional, species, atom_order, radial_widths,
          onsite_base, coupling, occupations):
    chips = lax.axis_size("chip")
    bands = lax.axis_size("band")
    swap = [(0, 1), (1, 0)]
    nb = wavefunctions.shape[2]
    owners = farthest_first([(i // 2, i % 2 * 2) for i in range(chips)], (chips // 2, 4), chips // 2 + 1)
    blocks = farthest_first([(i % (bands // 2), i * 2 // bands) for i in range(bands)], (bands // 2, 4), bands * 3 // 4)
    other, other_proj, own_row, grid, rhs = other_tables(
        owners, wavefunctions, miller, reciprocal, fractional, species, atom_order, radial_widths)
    received = lax.ppermute(other_proj, "core", swap)
    mine, mine_proj, couple, base_rows, weights = own_tables(
        bands, owners, own_row, grid, rhs, onsite_base.reshape(-1, 64), coupling, occupations.reshape(1, -1))
    chip_sum = (mine_proj + received.astype(F32)).astype(BF16).reshape(chips, -1, 2 * nb)
    parts = exchange(chip_sum, "chip", owners)

    proj, occupancy = occupancy_step(parts, weights, bands)
    occupancy = exchange(occupancy, "band", blocks)
    onsite, weighted = weigh(occupancy, proj, couple, base_rows, chips)
    weighted = exchange(weighted, "chip", owners).reshape(-1, 2 * nb)
    other_weighted = lax.ppermute(weighted, "core", swap)
    before, other_t, onsite = back(mine, weighted, other, onsite)
    applied = back_last(other_t, other_weighted, before)
    return applied, onsite


def solution(mesh):
    peers, bands = mesh.devices.shape
    inner = Mesh(mesh.devices.reshape(peers // 2, 2, bands), ("chip", "core", "band"))
    pw = ("chip", "core")
    placed = (P(None, pw, "band"), P(None, pw), P(), P(), P(), P(), P(), P(), P(), P("band"))
    return jax.shard_map(
        local,
        mesh=inner,
        in_specs=placed,
        out_specs=(P(None, pw, "band"), P(pw, None, None)),
        check_vma=False,
    )
```

```python
import functools
import math

import jax
import jax.numpy as jnp
from jax import lax
from jax.experimental import pallas as pl
from jax.experimental.pallas import tpu as pltpu
from jax.sharding import Mesh
from jax.sharding import PartitionSpec as P

HIGH = lax.Precision.HIGHEST
F32 = jnp.float32
BF16 = jnp.bfloat16
OTHER_ENDS = (10, 16)
OWN_ENDS = (14, 16)
CHUNKS = 4
SIN = (6.283185005187988, -41.341590881347656, 81.59994506835938,
       -76.61447143554688, 41.3428840637207, -12.471243858337402)
COS = (1.0, -19.73920440673828, 64.93911743164062, -85.45014190673828,
       60.16762924194336, -25.967599868774414, 6.528658390045166)
NT = (((1,), (1,)), ((), ()))
TN = (((0,), (0,)), ((), ()))
NN = (((1,), (0,)), ((), ()))


LIMIT = pltpu.CompilerParams(vmem_limit_bytes=16 << 20)


def dot_high(left, right, dims):
    return lax.dot_general(left, right, dims, precision=HIGH, preferred_element_type=F32)


def iota(shape, dim):
    return lax.broadcasted_iota(jnp.int32, shape, dim)


def in_parts(array):
    high = array.astype(BF16).astype(F32)
    rest = array - high
    middle = rest.astype(BF16).astype(F32)
    return high, middle, rest - middle


def gather_lanes(array, order):
    rows, lanes = array.shape
    parts = jnp.concatenate(in_parts(array), axis=0).astype(BF16)
    chosen = (iota((lanes, lanes), 0) == order).astype(F32).astype(BF16)
    picked = jnp.dot(parts, chosen, preferred_element_type=F32)
    return picked[:rows] + picked[rows:2 * rows] + picked[2 * rows:]


def horner(coefficients, z):
    total = jnp.full_like(z, coefficients[-1])
    for c in coefficients[-2::-1]:
        total = total * z + c
    return total


def vmem():
    return pl.BlockSpec(memory_space=pltpu.VMEM)


def hbm():
    return pl.BlockSpec(memory_space=pltpu.HBM)


def in_hbm(array):
    return pltpu.with_memory_space_constraint(array, pltpu.HBM)


def fetch(pairs, copied):
    copies = [pltpu.make_async_copy(src, dst, copied.at[k]) for k, (src, dst) in enumerate(pairs)]
    for copy in copies:
        copy.start()
    return copies


def project_rows(owners, by_row, grid_ref, rhs_ref, beta_ref, proj_ref, ends, before_first):
    done = 0
    gcount = grid_ref.shape[1]
    wide = (8, gcount)
    m, g = ([jnp.broadcast_to(grid_ref[d:d + 1, :], wide) for d in dims] for dims in ((0, 1, 2), (3, 4, 5)))
    g2 = jnp.broadcast_to(grid_ref[6:7, :], wide)
    first = iota(wide, 0) < 4
    pair_g = (None, jnp.where(first, g[0], g[1]), jnp.where(first, g[2], g[0]), jnp.where(first, g[1], g[2]))
    first1 = iota((8, 1), 0) < 4
    for q, chip in enumerate(owners):
        par = by_row[chip * 8:chip * 8 + 8, :]
        if q % 2 == 0:
            here = [par[:, k:k + 1] for k in range(3)]
            after = by_row[owners[q + 1] * 8:owners[q + 1] * 8 + 8, :]
            spot = [jnp.where(first1, here[k], after[:, k:k + 1]) for k in range(3)]
            turns = spot[0] * m[0] + spot[1] * m[1] + spot[2] * m[2]
            r = turns - jnp.round(turns)
            z = r * r
            both = [(v, pltpu.roll(v, 4, 0)) for v in (horner(SIN, z) * r, horner(COS, z))]
            sin, cos = (jnp.where(first, v, turned) for v, turned in both)
        else:
            sin, cos = (jnp.where(first, turned, v) for v, turned in both)
        minus_sin = -sin
        col = [par[:, k:k + 1] for k in range(7)]
        pair_w = (jnp.where(first1, col[3], col[4]), col[5], jnp.where(first1, col[5], col[6]), col[6])
        re, im = [], []
        for p in range(4):
            w = pair_w[p]
            decay = jnp.exp(g2 * (-0.5 * (w * w)))
            if p == 0:
                re.append(decay * cos)
                im.append(decay * minus_sin)
            else:
                amp = pair_g[p] * ((-w) * decay)
                re.append(amp * sin)
                im.append(amp * cos)
        beta_ref[q * 32:q * 32 + 32, 0:gcount] = jnp.concatenate(re, axis=0).astype(BF16)
        beta_ref[q * 32:q * 32 + 32, gcount:] = jnp.concatenate(im, axis=0).astype(BF16)
        if q + 1 in ends:
            if done == 0:
                before_first()
            rows = slice(done * 32, (q + 1) * 32)
            by_real = jnp.dot(beta_ref[rows, :gcount], rhs_ref[...], preferred_element_type=F32)
            by_imag = jnp.dot(beta_ref[rows, gcount:], rhs_ref[...], preferred_element_type=F32)
            half = rhs_ref.shape[1] // 2
            proj_ref[rows, :half] = (by_real[:, :half] + by_imag[:, half:]).astype(proj_ref.dtype)
            proj_ref[rows, half:] = (by_real[:, half:] - by_imag[:, :half]).astype(proj_ref.dtype)
            done = q + 1


def other_tables_kernel(owners, recip_hbm, widths_hbm, wave_hbm, miller_hbm, frac_hbm, species_hbm, order_hbm,
                        beta_ref, proj_ref, own_row_ref, grid_ref, rhs_ref,
                        recip_ref, widths_ref, wave_ref, miller_ref, frac_ref, species_ref, order_ref, copied):
    loads = fetch(((wave_hbm, wave_ref), (recip_hbm, recip_ref), (widths_hbm, widths_ref), (miller_hbm, miller_ref),
                   (frac_hbm, frac_ref), (species_hbm, species_ref), (order_hbm, order_ref)), copied)
    for load in loads[1:]:
        load.wait()
    core = lax.axis_index("core")
    gcount = miller_ref.shape[1]
    natoms = order_ref.shape[1]
    kinds = widths_ref.shape[0]
    spec = species_ref[...]
    rows = [frac_ref[d:d + 1, :] for d in range(3)]
    for c in range(4):
        row = jnp.zeros((1, natoms), F32)
        for s in range(kinds):
            row = jnp.where(spec == s, widths_ref[s:s + 1, c:c + 1], row)
        rows.append(row)
    rows.append(spec.astype(F32))
    by_slot = gather_lanes(jnp.concatenate(rows, axis=0), order_ref[...]).T
    low = iota((8, 8), 0) < 4
    first_four, last_four = [], []
    for q in range(len(owners)):
        here = by_slot[q * 8:q * 8 + 8, :]
        turned = pltpu.roll(here, 4, 0)
        first_four.append(jnp.where(low, here, turned))
        last_four.append(jnp.where(low, turned, here))
    first_four = jnp.concatenate(first_four, axis=0)
    last_four = jnp.concatenate(last_four, axis=0)
    by_row = jnp.where(core == 0, last_four, first_four)
    own_row_ref[...] = jnp.where(core == 0, first_four, last_four)

    mil = miller_ref[...].astype(F32)
    m = [mil[d:d + 1, :] for d in range(3)]
    two_pi = 2.0 * math.pi
    g = [two_pi * (recip_ref[d:d + 1, 0:1] * m[0] + recip_ref[d:d + 1, 1:2] * m[1] + recip_ref[d:d + 1, 2:3] * m[2])
         for d in range(3)]
    g2 = g[0] * g[0] + g[1] * g[1] + g[2] * g[2]
    grid_ref[...] = jnp.concatenate([*m, *g, g2, g2], axis=0)

    def make_rhs():
        loads[0].wait()
        nb = wave_ref.shape[2]
        rhs_ref[:, :nb] = wave_ref[0]
        rhs_ref[:, nb:] = wave_ref[1]

    project_rows(owners, by_row, grid_ref, rhs_ref, beta_ref, proj_ref, OTHER_ENDS, make_rhs)


def other_tables(owners, wavefunctions, miller, reciprocal, fractional, species, atom_order, radial_widths):
    gcount, nb = wavefunctions.shape[1:]
    natoms = atom_order.shape[0]
    args = (reciprocal, radial_widths, wavefunctions, miller, fractional, species.reshape(1, -1),
            atom_order.reshape(1, -1))
    return pl.pallas_call(
        functools.partial(other_tables_kernel, owners),
        out_shape=(jax.ShapeDtypeStruct((natoms * 4, 2 * gcount), BF16),
                   jax.ShapeDtypeStruct((natoms * 4, 2 * nb), BF16),
                   jax.ShapeDtypeStruct((natoms, 8), F32), jax.ShapeDtypeStruct((8, gcount), F32),
                   jax.ShapeDtypeStruct((gcount, 2 * nb), BF16)),
        in_specs=[hbm()] * len(args),
        out_specs=(vmem(),) * 5,
        scratch_shapes=[pltpu.VMEM(a.shape, a.dtype) for a in args] + [pltpu.SemaphoreType.DMA((len(args),))],
        compiler_params=LIMIT,
        name="other_tables",
    )(*(in_hbm(a) for a in args))


def own_tables_kernel(bands, owners, own_row_ref, grid_ref, rhs_ref, base_ref, coupling_hbm, occupations_hbm,
                      beta_ref, proj_ref, couple_ref, base_rows_ref, weights_ref,
                      coupling_ref, occupations_ref, copied):
    loads = fetch(((coupling_hbm, coupling_ref), (occupations_hbm, occupations_ref)), copied)
    chip = lax.axis_index("chip")

    def of_owned_atoms():
        for load in loads:
            load.wait()
        spec = own_row_ref[pl.ds(pl.multiple_of(chip * 8, 8), 8), 7:8]
        kinds = base_ref.shape[0]
        base = jnp.broadcast_to(base_ref[0:1, :], (8, 64))
        for s in range(1, kinds):
            base = jnp.where(spec == s, base_ref[s:s + 1, :], base)
        base_rows_ref[...] = base
        by_kind = [coupling_ref[s].T for s in range(kinds)]
        for a in range(4):
            for i in range(8):
                rows = slice(i * 8, i * 8 + 8)
                block = by_kind[0][rows]
                for s in range(1, kinds):
                    block = jnp.where(spec[a:a + 1, :] == s, by_kind[s][rows], block)
                to = ((i % 2) * 4 + i // 2) * 32 + a * 8
                couple_ref[to:to + 8, :] = block
        w = occupations_ref[...] * (1.0 / (occupations_ref.shape[1] * bands))
        weights_ref[...] = jnp.concatenate([w, w], axis=1)

    project_rows(owners, own_row_ref[...], grid_ref, rhs_ref, beta_ref, proj_ref, OWN_ENDS, of_owned_atoms)


def own_tables(bands, owners, own_row, grid, rhs, base, coupling, occupations):
    nrows = own_row.shape[0] * 4
    return pl.pallas_call(
        functools.partial(own_tables_kernel, bands, owners),
        out_shape=(jax.ShapeDtypeStruct((nrows, 2 * rhs.shape[0]), BF16), jax.ShapeDtypeStruct((nrows, rhs.shape[1]), F32),
                   jax.ShapeDtypeStruct((256, 64), F32), jax.ShapeDtypeStruct((8, 64), F32),
                   jax.ShapeDtypeStruct((1, rhs.shape[1]), F32)),
        in_specs=[vmem()] * 4 + [hbm()] * 2,
        out_specs=(vmem(),) * 5,
        scratch_shapes=[pltpu.VMEM(coupling.shape, F32), pltpu.VMEM(occupations.shape, F32),
                        pltpu.SemaphoreType.DMA((2,))],
        compiler_params=LIMIT,
        name="own_tables",
    )(own_row, grid, rhs, base, in_hbm(coupling), in_hbm(occupations))


def occupancy_kernel(parts_ref, weights_ref, proj_ref, send_ref):
    total = parts_ref[0].astype(F32)
    for k in range(1, parts_ref.shape[0]):
        total = total + parts_ref[k].astype(F32)
    nb = proj_ref.shape[2]
    proj_ref[0] = total[:, :nb]
    proj_ref[1] = total[:, nb:]
    by_atom = jnp.concatenate([jnp.concatenate(
        [proj_ref[h, pl.ds(a, 8, stride=4), :] for a in range(4)], axis=0) for h in range(2)], axis=1)
    gram = dot_high(total * weights_ref[...], by_atom, NT)
    flat = jnp.concatenate([gram[k * 8:k * 8 + 8, :] for k in range(4)], axis=1)
    flat = jnp.where((iota((8, 128), 1) // 8) % 4 == iota((8, 128), 0) % 4, flat, 0.0)
    flat = flat + pltpu.roll(flat, 1, 0)
    flat = flat + pltpu.roll(flat, 2, 0)
    flat = jnp.concatenate([flat[3:4, :], flat[7:8, :]], axis=0)
    for k in range(send_ref.shape[0]):
        send_ref[k] = flat


def occupancy_step(parts, weights, peers):
    _, nrows, width = parts.shape
    return pl.pallas_call(
        occupancy_kernel,
        out_shape=(jax.ShapeDtypeStruct((2, nrows, width // 2), F32), jax.ShapeDtypeStruct((peers, 2, 128), F32)),
        in_specs=[vmem(), vmem()],
        out_specs=(vmem(), vmem()),
        compiler_params=LIMIT,
        name="occupancy",
    )(parts, weights)


def weigh_kernel(parts_ref, proj_ref, couple_ref, base_ref, onsite_ref, send_ref):
    occ = parts_ref[0]
    for k in range(1, parts_ref.shape[0]):
        occ = occ + parts_ref[k]
    occ = jnp.concatenate([occ[0:1, :], occ[1:2, :]], axis=1)
    own_atom = (iota((8, 256), 1) // 8) % 4 == iota((8, 256), 0) % 4
    onsite = dot_high(jnp.where(own_atom, occ, 0.0), couple_ref[...], NN) + base_ref[...]
    onsite_ref[...] = onsite
    pair = jnp.where(iota((8, 64), 0) < 4, onsite, jnp.concatenate([onsite[:, 8:], onsite[:, :8]], axis=1))
    low = iota((8, 2 * proj_ref.shape[2]), 0) < 4
    total = [None] * 4
    for k in range(4):
        here = jnp.concatenate([proj_ref[h, k * 8:k * 8 + 8, :] for h in range(2)], axis=1)
        turned = pltpu.roll(here, 4, 0)
        for j, both in ((2 * k, jnp.where(low, here, turned)), (2 * k + 1, jnp.where(low, turned, here))):
            for t in range(4):
                term = pair[:, 16 * t + j:16 * t + j + 1] * both
                total[t] = term if total[t] is None else total[t] + term
    weighted = jnp.concatenate(total, axis=0).astype(BF16)
    for k in range(send_ref.shape[0]):
        send_ref[k] = weighted


def weigh(parts, proj, couple, base_rows, peers):
    return pl.pallas_call(
        weigh_kernel,
        out_shape=(jax.ShapeDtypeStruct((8, 64), F32), jax.ShapeDtypeStruct((peers, proj.shape[1], 2 * proj.shape[2]), BF16)),
        in_specs=[vmem()] * 4,
        out_specs=(vmem(), vmem()),
        compiler_params=LIMIT,
        name="weigh",
    )(parts, proj, couple, base_rows)


def turned_by_i(weighted):
    half = weighted.shape[1] // 2
    return jnp.concatenate([-weighted[:, half:], weighted[:, :half]], axis=1)


def back_kernel(table_ref, weighted_ref, other_ref, onsite_ref, out_ref, other_t_ref, square_ref):
    for i in range(8):
        square_ref[:, i, :] = onsite_ref[0:4, i * 8:i * 8 + 8]
    gcount = table_ref.shape[1] // 2
    weighted = weighted_ref[...]
    total = (lax.dot_general(weighted, table_ref[:, :gcount], TN, preferred_element_type=F32)
             + lax.dot_general(turned_by_i(weighted), table_ref[:, gcount:], TN, preferred_element_type=F32))
    out_ref[...] = total.T
    other_t_ref[0] = other_ref[:, :gcount].T
    other_t_ref[1] = other_ref[:, gcount:].T


def back(table, weighted, other, onsite):
    gcount = table.shape[1] // 2
    return pl.pallas_call(
        back_kernel,
        out_shape=(jax.ShapeDtypeStruct((gcount, weighted.shape[1]), F32),
                   jax.ShapeDtypeStruct((2, gcount, other.shape[0]), BF16), jax.ShapeDtypeStruct((4, 8, 8), F32)),
        in_specs=[vmem()] * 4, out_specs=(vmem(),) * 3, compiler_params=LIMIT, name="back",
    )(table, weighted, other, onsite)


def back_last_kernel(table_ref, weighted_ref, before_ref, out_hbm, out_ref, copied):
    half = weighted_ref.shape[1] // 2
    weighted = weighted_ref[...]
    chunks = copied.shape[0]
    size = table_ref.shape[1] // chunks
    copies = []
    for k in range(chunks):
        rows = slice(k * size, (k + 1) * size)
        by_real = jnp.dot(table_ref[0, rows, :], weighted, preferred_element_type=F32)
        by_imag = jnp.dot(table_ref[1, rows, :], weighted, preferred_element_type=F32)
        out_ref[k, 0] = (before_ref[rows, :half] + (by_real[:, :half] - by_imag[:, half:])).astype(BF16)
        out_ref[k, 1] = (before_ref[rows, half:] + (by_real[:, half:] + by_imag[:, :half])).astype(BF16)
        copies.append(pltpu.make_async_copy(out_ref.at[k], out_hbm.at[:, pl.ds(k * size, size), :], copied.at[k]))
        copies[-1].start()
    for copy in copies:
        copy.wait()


def back_last(table, weighted, before):
    gcount, width = before.shape
    return pl.pallas_call(
        back_last_kernel,
        out_shape=jax.ShapeDtypeStruct((2, gcount, width // 2), BF16),
        in_specs=[vmem()] * 3, out_specs=hbm(),
        scratch_shapes=[pltpu.VMEM((CHUNKS, 2, gcount // CHUNKS, width // 2), BF16),
                        pltpu.SemaphoreType.DMA((CHUNKS,))],
        compiler_params=LIMIT, name="back_last",
    )(table, weighted, before)


def farthest_first(places, extents, first):
    def distance(i):
        steps = [abs(a - b) for a, b in zip(places[i], places[first])]
        return sum(min(s, n - s) for s, n in zip(steps, extents))
    others = [i for i in range(len(places)) if i != first]
    return [first] + sorted(others, key=lambda i: (-distance(i), (i - first) % len(places)))


def exchange(blocks, axis, members):
    return lax.all_to_all(blocks, axis, 0, 0, axis_index_groups=[members], tiled=True)


def local(wavefunctions, miller, reciprocal, fractional, species, atom_order, radial_widths,
          onsite_base, coupling, occupations):
    chips = lax.axis_size("chip")
    bands = lax.axis_size("band")
    swap = [(0, 1), (1, 0)]
    nb = wavefunctions.shape[2]
    owners = farthest_first([(i // 2, i % 2 * 2) for i in range(chips)], (chips // 2, 4), chips // 2 + 1)
    blocks = farthest_first([(i % (bands // 2), i * 2 // bands) for i in range(bands)], (bands // 2, 4), bands * 3 // 4)
    other, other_proj, own_row, grid, rhs = other_tables(
        owners, wavefunctions, miller, reciprocal, fractional, species, atom_order, radial_widths)
    received = lax.ppermute(other_proj, "core", swap)
    mine, mine_proj, couple, base_rows, weights = own_tables(
        bands, owners, own_row, grid, rhs, onsite_base.reshape(-1, 64), coupling, occupations.reshape(1, -1))
    chip_sum = (mine_proj + received.astype(F32)).astype(BF16).reshape(chips, -1, 2 * nb)
    parts = exchange(chip_sum, "chip", owners)

    proj, occupancy = occupancy_step(parts, weights, bands)
    occupancy = exchange(occupancy, "band", blocks)
    onsite, weighted = weigh(occupancy, proj, couple, base_rows, chips)
    weighted = exchange(weighted, "chip", owners).reshape(-1, 2 * nb)
    other_weighted = lax.ppermute(weighted, "core", swap)
    before, other_t, onsite = back(mine, weighted, other, onsite)
    applied = back_last(other_t, other_weighted, before)
    return applied, onsite


def solution(mesh):
    peers, bands = mesh.devices.shape
    inner = Mesh(mesh.devices.reshape(peers // 2, 2, bands), ("chip", "core", "band"))
    pw = ("chip", "core")
    placed = (P(None, pw, "band"), P(None, pw), P(), P(), P(), P(), P(), P(), P(), P("band"))
    return jax.shard_map(
        local,
        mesh=inner,
        in_specs=placed,
        out_specs=(P(None, pw, "band"), P(pw, None, None)),
        check_vma=False,
    )
```

```python
import functools
import math

import jax
import jax.numpy as jnp
from jax import lax
from jax.experimental import pallas as pl
from jax.experimental.pallas import tpu as pltpu
from jax.sharding import Mesh
from jax.sharding import PartitionSpec as P

HIGH = lax.Precision.HIGHEST
F32 = jnp.float32
BF16 = jnp.bfloat16
OTHER_ENDS = (10, 16)
OWN_ENDS = (14, 16)
CHUNKS = 4
SIN = (6.283185005187988, -41.341590881347656, 81.59994506835938,
       -76.61447143554688, 41.3428840637207, -12.471243858337402)
COS = (1.0, -19.73920440673828, 64.93911743164062, -85.45014190673828,
       60.16762924194336, -25.967599868774414, 6.528658390045166)
NT = (((1,), (1,)), ((), ()))
TN = (((0,), (0,)), ((), ()))
NN = (((1,), (0,)), ((), ()))


LIMIT = pltpu.CompilerParams(vmem_limit_bytes=16 << 20)


def dot_high(left, right, dims):
    return lax.dot_general(left, right, dims, precision=HIGH, preferred_element_type=F32)


def iota(shape, dim):
    return lax.broadcasted_iota(jnp.int32, shape, dim)


def in_parts(array):
    high = array.astype(BF16).astype(F32)
    rest = array - high
    middle = rest.astype(BF16).astype(F32)
    return high, middle, rest - middle


def gather_lanes(array, order):
    rows, lanes = array.shape
    parts = jnp.concatenate(in_parts(array), axis=0).astype(BF16)
    chosen = (iota((lanes, lanes), 0) == order).astype(F32).astype(BF16)
    picked = jnp.dot(parts, chosen, preferred_element_type=F32)
    return picked[:rows] + picked[rows:2 * rows] + picked[2 * rows:]


def horner(coefficients, z):
    total = jnp.full_like(z, coefficients[-1])
    for c in coefficients[-2::-1]:
        total = total * z + c
    return total


def vmem():
    return pl.BlockSpec(memory_space=pltpu.VMEM)


def hbm():
    return pl.BlockSpec(memory_space=pltpu.HBM)


def in_hbm(array):
    return pltpu.with_memory_space_constraint(array, pltpu.HBM)


def fetch(pairs, copied):
    copies = [pltpu.make_async_copy(src, dst, copied.at[k]) for k, (src, dst) in enumerate(pairs)]
    for copy in copies:
        copy.start()
    return copies


def project_rows(owners, by_row, grid_ref, rhs_ref, beta_ref, proj_ref, ends, before_first):
    done = 0
    gcount = grid_ref.shape[1]
    wide = (8, gcount)
    m, g = ([jnp.broadcast_to(grid_ref[d:d + 1, :], wide) for d in dims] for dims in ((0, 1, 2), (3, 4, 5)))
    g2 = jnp.broadcast_to(grid_ref[6:7, :], wide)
    first = iota(wide, 0) < 4
    pair_g = (None, jnp.where(first, g[0], g[1]), jnp.where(first, g[2], g[0]), jnp.where(first, g[1], g[2]))
    first1 = iota((8, 1), 0) < 4
    for q, chip in enumerate(owners):
        par = by_row[chip * 8:chip * 8 + 8, :]
        if q % 2 == 0:
            here = [par[:, k:k + 1] for k in range(3)]
            after = by_row[owners[q + 1] * 8:owners[q + 1] * 8 + 8, :]
            spot = [jnp.where(first1, here[k], after[:, k:k + 1]) for k in range(3)]
            turns = spot[0] * m[0] + spot[1] * m[1] + spot[2] * m[2]
            r = turns - jnp.round(turns)
            z = r * r
            both = [(v, pltpu.roll(v, 4, 0)) for v in (horner(SIN, z) * r, horner(COS, z))]
            sin, cos = (jnp.where(first, v, turned) for v, turned in both)
        else:
            sin, cos = (jnp.where(first, turned, v) for v, turned in both)
        minus_sin = -sin
        col = [par[:, k:k + 1] for k in range(7)]
        pair_w = (jnp.where(first1, col[3], col[4]), col[5], jnp.where(first1, col[5], col[6]), col[6])
        re, im = [], []
        for p in range(4):
            w = pair_w[p]
            decay = jnp.exp(g2 * (-0.5 * (w * w)))
            if p == 0:
                re.append(decay * cos)
                im.append(decay * minus_sin)
            else:
                amp = pair_g[p] * ((-w) * decay)
                re.append(amp * sin)
                im.append(amp * cos)
        beta_ref[q * 32:q * 32 + 32, 0:gcount] = jnp.concatenate(re, axis=0).astype(BF16)
        beta_ref[q * 32:q * 32 + 32, gcount:] = jnp.concatenate(im, axis=0).astype(BF16)
        if q + 1 in ends:
            if done == 0:
                before_first()
            rows = slice(done * 32, (q + 1) * 32)
            by_real = jnp.dot(beta_ref[rows, :gcount], rhs_ref[...], preferred_element_type=F32)
            by_imag = jnp.dot(beta_ref[rows, gcount:], rhs_ref[...], preferred_element_type=F32)
            half = rhs_ref.shape[1] // 2
            proj_ref[rows, :half] = (by_real[:, :half] + by_imag[:, half:]).astype(proj_ref.dtype)
            proj_ref[rows, half:] = (by_real[:, half:] - by_imag[:, :half]).astype(proj_ref.dtype)
            done = q + 1


def other_tables_kernel(owners, recip_hbm, widths_hbm, wave_hbm, miller_hbm, frac_hbm, species_hbm, order_hbm,
                        beta_ref, proj_ref, own_row_ref, grid_ref, rhs_ref,
                        recip_ref, widths_ref, wave_ref, miller_ref, frac_ref, species_ref, order_ref, copied):
    *loads, wave_load = fetch(
        ((order_hbm, order_ref), (species_hbm, species_ref), (widths_hbm, widths_ref), (frac_hbm, frac_ref),
         (recip_hbm, recip_ref), (miller_hbm, miller_ref), (wave_hbm, wave_ref)), copied)
    for load in loads:
        load.wait()
    core = lax.axis_index("core")
    gcount = miller_ref.shape[1]
    natoms = order_ref.shape[1]
    kinds = widths_ref.shape[0]
    spec = species_ref[...]
    rows = [frac_ref[d:d + 1, :] for d in range(3)]
    for c in range(4):
        row = jnp.zeros((1, natoms), F32)
        for s in range(kinds):
            row = jnp.where(spec == s, widths_ref[s:s + 1, c:c + 1], row)
        rows.append(row)
    rows.append(spec.astype(F32))
    by_slot = gather_lanes(jnp.concatenate(rows, axis=0), order_ref[...]).T
    low = iota((8, 8), 0) < 4
    first_four, last_four = [], []
    for q in range(len(owners)):
        here = by_slot[q * 8:q * 8 + 8, :]
        turned = pltpu.roll(here, 4, 0)
        first_four.append(jnp.where(low, here, turned))
        last_four.append(jnp.where(low, turned, here))
    first_four = jnp.concatenate(first_four, axis=0)
    last_four = jnp.concatenate(last_four, axis=0)
    by_row = jnp.where(core == 0, last_four, first_four)
    own_row_ref[...] = jnp.where(core == 0, first_four, last_four)

    mil = miller_ref[...].astype(F32)
    m = [mil[d:d + 1, :] for d in range(3)]
    two_pi = 2.0 * math.pi
    g = [two_pi * (recip_ref[d:d + 1, 0:1] * m[0] + recip_ref[d:d + 1, 1:2] * m[1] + recip_ref[d:d + 1, 2:3] * m[2])
         for d in range(3)]
    g2 = g[0] * g[0] + g[1] * g[1] + g[2] * g[2]
    grid_ref[...] = jnp.concatenate([*m, *g, g2, g2], axis=0)

    def make_rhs():
        wave_load.wait()
        nb = wave_ref.shape[2]
        rhs_ref[:, :nb] = wave_ref[0]
        rhs_ref[:, nb:] = wave_ref[1]

    project_rows(owners, by_row, grid_ref, rhs_ref, beta_ref, proj_ref, OTHER_ENDS, make_rhs)


def other_tables(owners, wavefunctions, miller, reciprocal, fractional, species, atom_order, radial_widths):
    gcount, nb = wavefunctions.shape[1:]
    natoms = atom_order.shape[0]
    args = (reciprocal, radial_widths, wavefunctions, miller, fractional, species.reshape(1, -1),
            atom_order.reshape(1, -1))
    return pl.pallas_call(
        functools.partial(other_tables_kernel, owners),
        out_shape=(jax.ShapeDtypeStruct((natoms * 4, 2 * gcount), BF16),
                   jax.ShapeDtypeStruct((natoms * 4, 2 * nb), BF16),
                   jax.ShapeDtypeStruct((natoms, 8), F32), jax.ShapeDtypeStruct((8, gcount), F32),
                   jax.ShapeDtypeStruct((gcount, 2 * nb), BF16)),
        in_specs=[hbm()] * len(args),
        out_specs=(vmem(),) * 5,
        scratch_shapes=[pltpu.VMEM(a.shape, a.dtype) for a in args] + [pltpu.SemaphoreType.DMA((len(args),))],
        compiler_params=LIMIT,
        name="other_tables",
    )(*(in_hbm(a) for a in args))


def own_tables_kernel(bands, owners, own_row_ref, grid_ref, rhs_ref, base_ref, coupling_hbm, occupations_hbm,
                      beta_ref, proj_ref, couple_ref, base_rows_ref, weights_ref,
                      coupling_ref, occupations_ref, copied):
    loads = fetch(((coupling_hbm, coupling_ref), (occupations_hbm, occupations_ref)), copied)
    chip = lax.axis_index("chip")

    def of_owned_atoms():
        for load in loads:
            load.wait()
        spec = own_row_ref[pl.ds(pl.multiple_of(chip * 8, 8), 8), 7:8]
        kinds = base_ref.shape[0]
        base = jnp.broadcast_to(base_ref[0:1, :], (8, 64))
        for s in range(1, kinds):
            base = jnp.where(spec == s, base_ref[s:s + 1, :], base)
        base_rows_ref[...] = base
        by_kind = [coupling_ref[s].T for s in range(kinds)]
        for a in range(4):
            for i in range(8):
                rows = slice(i * 8, i * 8 + 8)
                block = by_kind[0][rows]
                for s in range(1, kinds):
                    block = jnp.where(spec[a:a + 1, :] == s, by_kind[s][rows], block)
                to = ((i % 2) * 4 + i // 2) * 32 + a * 8
                couple_ref[to:to + 8, :] = block
        w = occupations_ref[...] * (1.0 / (occupations_ref.shape[1] * bands))
        weights_ref[...] = jnp.concatenate([w, w], axis=1)

    project_rows(owners, own_row_ref[...], grid_ref, rhs_ref, beta_ref, proj_ref, OWN_ENDS, of_owned_atoms)


def own_tables(bands, owners, own_row, grid, rhs, base, coupling, occupations):
    nrows = own_row.shape[0] * 4
    return pl.pallas_call(
        functools.partial(own_tables_kernel, bands, owners),
        out_shape=(jax.ShapeDtypeStruct((nrows, 2 * rhs.shape[0]), BF16), jax.ShapeDtypeStruct((nrows, rhs.shape[1]), F32),
                   jax.ShapeDtypeStruct((256, 64), F32), jax.ShapeDtypeStruct((8, 64), F32),
                   jax.ShapeDtypeStruct((1, rhs.shape[1]), F32)),
        in_specs=[vmem()] * 4 + [hbm()] * 2,
        out_specs=(vmem(),) * 5,
        scratch_shapes=[pltpu.VMEM(coupling.shape, F32), pltpu.VMEM(occupations.shape, F32),
                        pltpu.SemaphoreType.DMA((2,))],
        compiler_params=LIMIT,
        name="own_tables",
    )(own_row, grid, rhs, base, in_hbm(coupling), in_hbm(occupations))


def occupancy_kernel(parts_ref, weights_ref, proj_ref, send_ref):
    total = parts_ref[0].astype(F32)
    for k in range(1, parts_ref.shape[0]):
        total = total + parts_ref[k].astype(F32)
    nb = proj_ref.shape[2]
    proj_ref[0] = total[:, :nb]
    proj_ref[1] = total[:, nb:]
    by_atom = jnp.concatenate([jnp.concatenate(
        [proj_ref[h, pl.ds(a, 8, stride=4), :] for a in range(4)], axis=0) for h in range(2)], axis=1)
    gram = dot_high(total * weights_ref[...], by_atom, NT)
    flat = jnp.concatenate([gram[k * 8:k * 8 + 8, :] for k in range(4)], axis=1)
    flat = jnp.where((iota((8, 128), 1) // 8) % 4 == iota((8, 128), 0) % 4, flat, 0.0)
    flat = flat + pltpu.roll(flat, 1, 0)
    flat = flat + pltpu.roll(flat, 2, 0)
    flat = jnp.concatenate([flat[3:4, :], flat[7:8, :]], axis=0)
    for k in range(send_ref.shape[0]):
        send_ref[k] = flat


def occupancy_step(parts, weights, peers):
    _, nrows, width = parts.shape
    return pl.pallas_call(
        occupancy_kernel,
        out_shape=(jax.ShapeDtypeStruct((2, nrows, width // 2), F32), jax.ShapeDtypeStruct((peers, 2, 128), F32)),
        in_specs=[vmem(), vmem()],
        out_specs=(vmem(), vmem()),
        compiler_params=LIMIT,
        name="occupancy",
    )(parts, weights)


def weigh_kernel(parts_ref, proj_ref, couple_ref, base_ref, onsite_ref, send_ref):
    occ = parts_ref[0]
    for k in range(1, parts_ref.shape[0]):
        occ = occ + parts_ref[k]
    occ = jnp.concatenate([occ[0:1, :], occ[1:2, :]], axis=1)
    own_atom = (iota((8, 256), 1) // 8) % 4 == iota((8, 256), 0) % 4
    onsite = dot_high(jnp.where(own_atom, occ, 0.0), couple_ref[...], NN) + base_ref[...]
    onsite_ref[...] = onsite
    pair = jnp.where(iota((8, 64), 0) < 4, onsite, jnp.concatenate([onsite[:, 8:], onsite[:, :8]], axis=1))
    low = iota((8, 2 * proj_ref.shape[2]), 0) < 4
    total = [None] * 4
    for k in range(4):
        here = jnp.concatenate([proj_ref[h, k * 8:k * 8 + 8, :] for h in range(2)], axis=1)
        turned = pltpu.roll(here, 4, 0)
        for j, both in ((2 * k, jnp.where(low, here, turned)), (2 * k + 1, jnp.where(low, turned, here))):
            for t in range(4):
                term = pair[:, 16 * t + j:16 * t + j + 1] * both
                total[t] = term if total[t] is None else total[t] + term
    weighted = jnp.concatenate(total, axis=0).astype(BF16)
    for k in range(send_ref.shape[0]):
        send_ref[k] = weighted


def weigh(parts, proj, couple, base_rows, peers):
    return pl.pallas_call(
        weigh_kernel,
        out_shape=(jax.ShapeDtypeStruct((8, 64), F32), jax.ShapeDtypeStruct((peers, proj.shape[1], 2 * proj.shape[2]), BF16)),
        in_specs=[vmem()] * 4,
        out_specs=(vmem(), vmem()),
        compiler_params=LIMIT,
        name="weigh",
    )(parts, proj, couple, base_rows)


def turned_by_i(weighted):
    half = weighted.shape[1] // 2
    return jnp.concatenate([-weighted[:, half:], weighted[:, :half]], axis=1)


def back_kernel(table_ref, weighted_ref, other_ref, onsite_ref, out_ref, other_t_ref, square_ref):
    for i in range(8):
        square_ref[:, i, :] = onsite_ref[0:4, i * 8:i * 8 + 8]
    gcount = table_ref.shape[1] // 2
    weighted = weighted_ref[...]
    total = (lax.dot_general(weighted, table_ref[:, :gcount], TN, preferred_element_type=F32)
             + lax.dot_general(turned_by_i(weighted), table_ref[:, gcount:], TN, preferred_element_type=F32))
    out_ref[...] = total.T
    other_t_ref[0] = other_ref[:, :gcount].T
    other_t_ref[1] = other_ref[:, gcount:].T


def back(table, weighted, other, onsite):
    gcount = table.shape[1] // 2
    return pl.pallas_call(
        back_kernel,
        out_shape=(jax.ShapeDtypeStruct((gcount, weighted.shape[1]), F32),
                   jax.ShapeDtypeStruct((2, gcount, other.shape[0]), BF16), jax.ShapeDtypeStruct((4, 8, 8), F32)),
        in_specs=[vmem()] * 4, out_specs=(vmem(),) * 3, compiler_params=LIMIT, name="back",
    )(table, weighted, other, onsite)


def back_last_kernel(table_ref, weighted_ref, before_ref, out_hbm, out_ref, copied):
    half = weighted_ref.shape[1] // 2
    weighted = weighted_ref[...]
    chunks = copied.shape[0]
    size = table_ref.shape[1] // chunks
    copies = []
    for k in range(chunks):
        rows = slice(k * size, (k + 1) * size)
        by_real = jnp.dot(table_ref[0, rows, :], weighted, preferred_element_type=F32)
        by_imag = jnp.dot(table_ref[1, rows, :], weighted, preferred_element_type=F32)
        out_ref[k, 0] = (before_ref[rows, :half] + (by_real[:, :half] - by_imag[:, half:])).astype(BF16)
        out_ref[k, 1] = (before_ref[rows, half:] + (by_real[:, half:] + by_imag[:, :half])).astype(BF16)
        copies.append(pltpu.make_async_copy(out_ref.at[k], out_hbm.at[:, pl.ds(k * size, size), :], copied.at[k]))
        copies[-1].start()
    for copy in copies:
        copy.wait()


def back_last(table, weighted, before):
    gcount, width = before.shape
    return pl.pallas_call(
        back_last_kernel,
        out_shape=jax.ShapeDtypeStruct((2, gcount, width // 2), BF16),
        in_specs=[vmem()] * 3, out_specs=hbm(),
        scratch_shapes=[pltpu.VMEM((CHUNKS, 2, gcount // CHUNKS, width // 2), BF16),
                        pltpu.SemaphoreType.DMA((CHUNKS,))],
        compiler_params=LIMIT, name="back_last",
    )(table, weighted, before)


def farthest_first(places, extents, first):
    def distance(i):
        steps = [abs(a - b) for a, b in zip(places[i], places[first])]
        return sum(min(s, n - s) for s, n in zip(steps, extents))
    others = [i for i in range(len(places)) if i != first]
    return [first] + sorted(others, key=lambda i: (-distance(i), (i - first) % len(places)))


def exchange(blocks, axis, members):
    return lax.all_to_all(blocks, axis, 0, 0, axis_index_groups=[members], tiled=True)


def local(wavefunctions, miller, reciprocal, fractional, species, atom_order, radial_widths,
          onsite_base, coupling, occupations):
    chips = lax.axis_size("chip")
    bands = lax.axis_size("band")
    swap = [(0, 1), (1, 0)]
    nb = wavefunctions.shape[2]
    owners = farthest_first([(i // 2, i % 2 * 2) for i in range(chips)], (chips // 2, 4), chips * 3 // 4 + 1)
    blocks = farthest_first([(i % (bands // 2), i * 2 // bands) for i in range(bands)], (bands // 2, 4), bands * 3 // 4 + 1)
    other, other_proj, own_row, grid, rhs = other_tables(
        owners, wavefunctions, miller, reciprocal, fractional, species, atom_order, radial_widths)
    received = lax.ppermute(other_proj, "core", swap)
    mine, mine_proj, couple, base_rows, weights = own_tables(
        bands, owners, own_row, grid, rhs, onsite_base.reshape(-1, 64), coupling, occupations.reshape(1, -1))
    chip_sum = (mine_proj + received.astype(F32)).astype(BF16).reshape(chips, -1, 2 * nb)
    parts = exchange(chip_sum, "chip", owners)

    proj, occupancy = occupancy_step(parts, weights, bands)
    occupancy = exchange(occupancy, "band", blocks)
    onsite, weighted = weigh(occupancy, proj, couple, base_rows, chips)
    weighted = exchange(weighted, "chip", owners).reshape(-1, 2 * nb)
    other_weighted = lax.ppermute(weighted, "core", swap)
    before, other_t, onsite = back(mine, weighted, other, onsite)
    applied = back_last(other_t, other_weighted, before)
    return applied, onsite


def solution(mesh):
    peers, bands = mesh.devices.shape
    inner = Mesh(mesh.devices.reshape(peers // 2, 2, bands), ("chip", "core", "band"))
    pw = ("chip", "core")
    placed = (P(None, pw, "band"), P(None, pw), P(), P(), P(), P(), P(), P(), P(), P("band"))
    return jax.shard_map(
        local,
        mesh=inner,
        in_specs=placed,
        out_specs=(P(None, pw, "band"), P(pw, None, None)),
        check_vma=False,
    )
```

```python
import functools
import math

import jax
import jax.numpy as jnp
from jax import lax
from jax.experimental import pallas as pl
from jax.experimental.pallas import tpu as pltpu
from jax.sharding import Mesh
from jax.sharding import PartitionSpec as P

HIGH = lax.Precision.HIGHEST
F32 = jnp.float32
BF16 = jnp.bfloat16
OTHER_ENDS = (10, 16)
OWN_ENDS = (14, 16)
CHUNKS = 4
SIN = (6.283185005187988, -41.341590881347656, 81.59994506835938,
       -76.61447143554688, 41.3428840637207, -12.471243858337402)
COS = (1.0, -19.73920440673828, 64.93911743164062, -85.45014190673828,
       60.16762924194336, -25.967599868774414, 6.528658390045166)
NT = (((1,), (1,)), ((), ()))
TN = (((0,), (0,)), ((), ()))
NN = (((1,), (0,)), ((), ()))


LIMIT = pltpu.CompilerParams(vmem_limit_bytes=16 << 20)


def dot_high(left, right, dims):
    return lax.dot_general(left, right, dims, precision=HIGH, preferred_element_type=F32)


def iota(shape, dim):
    return lax.broadcasted_iota(jnp.int32, shape, dim)


def in_parts(array):
    high = array.astype(BF16).astype(F32)
    rest = array - high
    middle = rest.astype(BF16).astype(F32)
    return high, middle, rest - middle


def gather_lanes(array, order):
    rows, lanes = array.shape
    parts = jnp.concatenate(in_parts(array), axis=0).astype(BF16)
    chosen = (iota((lanes, lanes), 0) == order).astype(F32).astype(BF16)
    picked = jnp.dot(parts, chosen, preferred_element_type=F32)
    return picked[:rows] + picked[rows:2 * rows] + picked[2 * rows:]


def horner(coefficients, z):
    total = jnp.full_like(z, coefficients[-1])
    for c in coefficients[-2::-1]:
        total = total * z + c
    return total


def vmem():
    return pl.BlockSpec(memory_space=pltpu.VMEM)


def hbm():
    return pl.BlockSpec(memory_space=pltpu.HBM)


def in_hbm(array):
    return pltpu.with_memory_space_constraint(array, pltpu.HBM)


def fetch(pairs, copied):
    copies = [pltpu.make_async_copy(src, dst, copied.at[k]) for k, (src, dst) in enumerate(pairs)]
    for copy in copies:
        copy.start()
    return copies


def project_rows(owners, by_row, grid_ref, rhs_ref, beta_ref, proj_ref, ends, before_first):
    done = 0
    gcount = grid_ref.shape[1]
    wide = (8, gcount)
    m, g = ([jnp.broadcast_to(grid_ref[d:d + 1, :], wide) for d in dims] for dims in ((0, 1, 2), (3, 4, 5)))
    g2 = jnp.broadcast_to(grid_ref[6:7, :], wide)
    first = iota(wide, 0) < 4
    pair_g = (None, jnp.where(first, g[0], g[1]), jnp.where(first, g[2], g[0]), jnp.where(first, g[1], g[2]))
    first1 = iota((8, 1), 0) < 4
    for q, chip in enumerate(owners):
        par = by_row[chip * 8:chip * 8 + 8, :]
        if q % 2 == 0:
            here = [par[:, k:k + 1] for k in range(3)]
            after = by_row[owners[q + 1] * 8:owners[q + 1] * 8 + 8, :]
            spot = [jnp.where(first1, here[k], after[:, k:k + 1]) for k in range(3)]
            turns = spot[0] * m[0] + spot[1] * m[1] + spot[2] * m[2]
            r = turns - jnp.round(turns)
            z = r * r
            both = [(v, pltpu.roll(v, 4, 0)) for v in (horner(SIN, z) * r, horner(COS, z))]
            sin, cos = (jnp.where(first, v, turned) for v, turned in both)
        else:
            sin, cos = (jnp.where(first, turned, v) for v, turned in both)
        minus_sin = -sin
        col = [par[:, k:k + 1] for k in range(7)]
        pair_w = (jnp.where(first1, col[3], col[4]), col[5], jnp.where(first1, col[5], col[6]), col[6])
        re, im = [], []
        for p in range(4):
            w = pair_w[p]
            decay = jnp.exp(g2 * (-0.5 * (w * w)))
            if p == 0:
                re.append(decay * cos)
                im.append(decay * minus_sin)
            else:
                amp = pair_g[p] * ((-w) * decay)
                re.append(amp * sin)
                im.append(amp * cos)
        beta_ref[q * 32:q * 32 + 32, 0:gcount] = jnp.concatenate(re, axis=0).astype(BF16)
        beta_ref[q * 32:q * 32 + 32, gcount:] = jnp.concatenate(im, axis=0).astype(BF16)
        if q + 1 in ends:
            if done == 0:
                before_first()
            rows = slice(done * 32, (q + 1) * 32)
            by_real = jnp.dot(beta_ref[rows, :gcount], rhs_ref[...], preferred_element_type=F32)
            by_imag = jnp.dot(beta_ref[rows, gcount:], rhs_ref[...], preferred_element_type=F32)
            half = rhs_ref.shape[1] // 2
            proj_ref[rows, :half] = (by_real[:, :half] + by_imag[:, half:]).astype(proj_ref.dtype)
            proj_ref[rows, half:] = (by_real[:, half:] - by_imag[:, :half]).astype(proj_ref.dtype)
            done = q + 1


def other_tables_kernel(owners, recip_hbm, widths_hbm, wave_hbm, miller_hbm, frac_hbm, species_hbm, order_hbm,
                        beta_ref, proj_ref, own_row_ref, grid_ref, rhs_ref,
                        recip_ref, widths_ref, wave_ref, miller_ref, frac_ref, species_ref, order_ref, copied):
    *loads, wave_load = fetch(
        ((order_hbm, order_ref), (species_hbm, species_ref), (widths_hbm, widths_ref), (frac_hbm, frac_ref),
         (recip_hbm, recip_ref), (miller_hbm, miller_ref), (wave_hbm, wave_ref)), copied)
    for load in loads:
        load.wait()
    core = lax.axis_index("core")
    gcount = miller_ref.shape[1]
    natoms = order_ref.shape[1]
    kinds = widths_ref.shape[0]
    spec = species_ref[...]
    rows = [frac_ref[d:d + 1, :] for d in range(3)]
    for c in range(4):
        row = jnp.zeros((1, natoms), F32)
        for s in range(kinds):
            row = jnp.where(spec == s, widths_ref[s:s + 1, c:c + 1], row)
        rows.append(row)
    rows.append(spec.astype(F32))
    by_slot = gather_lanes(jnp.concatenate(rows, axis=0), order_ref[...]).T
    low = iota((8, 8), 0) < 4
    first_four, last_four = [], []
    for q in range(len(owners)):
        here = by_slot[q * 8:q * 8 + 8, :]
        turned = pltpu.roll(here, 4, 0)
        first_four.append(jnp.where(low, here, turned))
        last_four.append(jnp.where(low, turned, here))
    first_four = jnp.concatenate(first_four, axis=0)
    last_four = jnp.concatenate(last_four, axis=0)
    by_row = jnp.where(core == 0, last_four, first_four)
    own_row_ref[...] = jnp.where(core == 0, first_four, last_four)

    mil = miller_ref[...].astype(F32)
    m = [mil[d:d + 1, :] for d in range(3)]
    two_pi = 2.0 * math.pi
    g = [two_pi * (recip_ref[d:d + 1, 0:1] * m[0] + recip_ref[d:d + 1, 1:2] * m[1] + recip_ref[d:d + 1, 2:3] * m[2])
         for d in range(3)]
    g2 = g[0] * g[0] + g[1] * g[1] + g[2] * g[2]
    grid_ref[...] = jnp.concatenate([*m, *g, g2, g2], axis=0)

    def make_rhs():
        wave_load.wait()
        nb = wave_ref.shape[2]
        rhs_ref[:, :nb] = wave_ref[0]
        rhs_ref[:, nb:] = wave_ref[1]

    project_rows(owners, by_row, grid_ref, rhs_ref, beta_ref, proj_ref, OTHER_ENDS, make_rhs)


def other_tables(owners, wavefunctions, miller, reciprocal, fractional, species, atom_order, radial_widths):
    gcount, nb = wavefunctions.shape[1:]
    natoms = atom_order.shape[0]
    args = (reciprocal, radial_widths, wavefunctions, miller, fractional, species.reshape(1, -1),
            atom_order.reshape(1, -1))
    return pl.pallas_call(
        functools.partial(other_tables_kernel, owners),
        out_shape=(jax.ShapeDtypeStruct((natoms * 4, 2 * gcount), BF16),
                   jax.ShapeDtypeStruct((natoms * 4, 2 * nb), BF16),
                   jax.ShapeDtypeStruct((natoms, 8), F32), jax.ShapeDtypeStruct((8, gcount), F32),
                   jax.ShapeDtypeStruct((gcount, 2 * nb), BF16)),
        in_specs=[hbm()] * len(args),
        out_specs=(vmem(),) * 5,
        scratch_shapes=[pltpu.VMEM(a.shape, a.dtype) for a in args] + [pltpu.SemaphoreType.DMA((len(args),))],
        compiler_params=LIMIT,
        name="other_tables",
    )(*(in_hbm(a) for a in args))


def own_tables_kernel(bands, owners, own_row_ref, grid_ref, rhs_ref, base_hbm, coupling_hbm, occupations_hbm,
                      beta_ref, proj_ref, couple_ref, base_rows_ref, weights_ref,
                      base_ref, coupling_ref, occupations_ref, copied):
    loads = fetch(((coupling_hbm, coupling_ref), (occupations_hbm, occupations_ref), (base_hbm, base_ref)), copied)
    chip = lax.axis_index("chip")

    def of_owned_atoms():
        for load in loads:
            load.wait()
        spec = own_row_ref[pl.ds(pl.multiple_of(chip * 8, 8), 8), 7:8]
        kinds = base_ref.shape[0]
        flat = [jnp.concatenate([base_ref[s, i:i + 1, :] for i in range(8)], axis=1) for s in range(kinds)]
        base = jnp.broadcast_to(flat[0], (8, 64))
        for s in range(1, kinds):
            base = jnp.where(spec == s, flat[s], base)
        base_rows_ref[...] = base
        by_kind = [coupling_ref[s].T for s in range(kinds)]
        for a in range(4):
            for i in range(8):
                rows = slice(i * 8, i * 8 + 8)
                block = by_kind[0][rows]
                for s in range(1, kinds):
                    block = jnp.where(spec[a:a + 1, :] == s, by_kind[s][rows], block)
                to = ((i % 2) * 4 + i // 2) * 32 + a * 8
                couple_ref[to:to + 8, :] = block
        w = occupations_ref[...] * (1.0 / (occupations_ref.shape[1] * bands))
        weights_ref[...] = jnp.concatenate([w, w], axis=1)

    project_rows(owners, own_row_ref[...], grid_ref, rhs_ref, beta_ref, proj_ref, OWN_ENDS, of_owned_atoms)


def own_tables(bands, owners, own_row, grid, rhs, base, coupling, occupations):
    nrows = own_row.shape[0] * 4
    return pl.pallas_call(
        functools.partial(own_tables_kernel, bands, owners),
        out_shape=(jax.ShapeDtypeStruct((nrows, 2 * rhs.shape[0]), BF16), jax.ShapeDtypeStruct((nrows, rhs.shape[1]), F32),
                   jax.ShapeDtypeStruct((256, 64), F32), jax.ShapeDtypeStruct((8, 64), F32),
                   jax.ShapeDtypeStruct((1, rhs.shape[1]), F32)),
        in_specs=[vmem()] * 3 + [hbm()] * 3,
        out_specs=(vmem(),) * 5,
        scratch_shapes=[pltpu.VMEM(base.shape, F32), pltpu.VMEM(coupling.shape, F32),
                        pltpu.VMEM(occupations.shape, F32), pltpu.SemaphoreType.DMA((3,))],
        compiler_params=LIMIT,
        name="own_tables",
    )(own_row, grid, rhs, in_hbm(base), in_hbm(coupling), in_hbm(occupations))


def occupancy_kernel(parts_ref, weights_ref, proj_ref, send_ref):
    total = parts_ref[0].astype(F32)
    for k in range(1, parts_ref.shape[0]):
        total = total + parts_ref[k].astype(F32)
    nb = proj_ref.shape[2]
    proj_ref[0] = total[:, :nb]
    proj_ref[1] = total[:, nb:]
    by_atom = jnp.concatenate([jnp.concatenate(
        [proj_ref[h, pl.ds(a, 8, stride=4), :] for a in range(4)], axis=0) for h in range(2)], axis=1)
    gram = dot_high(total * weights_ref[...], by_atom, NT)
    flat = jnp.concatenate([gram[k * 8:k * 8 + 8, :] for k in range(4)], axis=1)
    flat = jnp.where((iota((8, 128), 1) // 8) % 4 == iota((8, 128), 0) % 4, flat, 0.0)
    flat = flat + pltpu.roll(flat, 1, 0)
    flat = flat + pltpu.roll(flat, 2, 0)
    flat = jnp.concatenate([flat[3:4, :], flat[7:8, :]], axis=0)
    for k in range(send_ref.shape[0]):
        send_ref[k] = flat


def occupancy_step(parts, weights, peers):
    _, nrows, width = parts.shape
    return pl.pallas_call(
        occupancy_kernel,
        out_shape=(jax.ShapeDtypeStruct((2, nrows, width // 2), F32), jax.ShapeDtypeStruct((peers, 2, 128), F32)),
        in_specs=[vmem(), vmem()],
        out_specs=(vmem(), vmem()),
        compiler_params=LIMIT,
        name="occupancy",
    )(parts, weights)


def weigh_kernel(parts_ref, proj_ref, couple_ref, base_ref, onsite_ref, send_ref):
    occ = parts_ref[0]
    for k in range(1, parts_ref.shape[0]):
        occ = occ + parts_ref[k]
    occ = jnp.concatenate([occ[0:1, :], occ[1:2, :]], axis=1)
    own_atom = (iota((8, 256), 1) // 8) % 4 == iota((8, 256), 0) % 4
    onsite = dot_high(jnp.where(own_atom, occ, 0.0), couple_ref[...], NN) + base_ref[...]
    onsite_ref[...] = onsite
    pair = jnp.where(iota((8, 64), 0) < 4, onsite, jnp.concatenate([onsite[:, 8:], onsite[:, :8]], axis=1))
    low = iota((8, 2 * proj_ref.shape[2]), 0) < 4
    total = [None] * 4
    for k in range(4):
        here = jnp.concatenate([proj_ref[h, k * 8:k * 8 + 8, :] for h in range(2)], axis=1)
        turned = pltpu.roll(here, 4, 0)
        for j, both in ((2 * k, jnp.where(low, here, turned)), (2 * k + 1, jnp.where(low, turned, here))):
            for t in range(4):
                term = pair[:, 16 * t + j:16 * t + j + 1] * both
                total[t] = term if total[t] is None else total[t] + term
    weighted = jnp.concatenate(total, axis=0).astype(BF16)
    for k in range(send_ref.shape[0]):
        send_ref[k] = weighted


def weigh(parts, proj, couple, base_rows, peers):
    return pl.pallas_call(
        weigh_kernel,
        out_shape=(jax.ShapeDtypeStruct((8, 64), F32), jax.ShapeDtypeStruct((peers, proj.shape[1], 2 * proj.shape[2]), BF16)),
        in_specs=[vmem()] * 4,
        out_specs=(vmem(), vmem()),
        compiler_params=LIMIT,
        name="weigh",
    )(parts, proj, couple, base_rows)


def turned_by_i(weighted):
    half = weighted.shape[1] // 2
    return jnp.concatenate([-weighted[:, half:], weighted[:, :half]], axis=1)


def back_kernel(table_ref, weighted_ref, other_ref, onsite_ref, out_ref, other_t_ref, square_ref):
    for i in range(8):
        square_ref[:, i, :] = onsite_ref[0:4, i * 8:i * 8 + 8]
    gcount = table_ref.shape[1] // 2
    weighted = weighted_ref[...]
    total = (lax.dot_general(weighted, table_ref[:, :gcount], TN, preferred_element_type=F32)
             + lax.dot_general(turned_by_i(weighted), table_ref[:, gcount:], TN, preferred_element_type=F32))
    out_ref[...] = total.T
    other_t_ref[0] = other_ref[:, :gcount].T
    other_t_ref[1] = other_ref[:, gcount:].T


def back(table, weighted, other, onsite):
    gcount = table.shape[1] // 2
    return pl.pallas_call(
        back_kernel,
        out_shape=(jax.ShapeDtypeStruct((gcount, weighted.shape[1]), F32),
                   jax.ShapeDtypeStruct((2, gcount, other.shape[0]), BF16), jax.ShapeDtypeStruct((4, 8, 8), F32)),
        in_specs=[vmem()] * 4, out_specs=(vmem(),) * 3, compiler_params=LIMIT, name="back",
    )(table, weighted, other, onsite)


def back_last_kernel(table_ref, weighted_ref, before_ref, out_hbm, out_ref, copied):
    half = weighted_ref.shape[1] // 2
    weighted = weighted_ref[...]
    chunks = copied.shape[0]
    size = table_ref.shape[1] // chunks
    copies = []
    for k in range(chunks):
        rows = slice(k * size, (k + 1) * size)
        by_real = jnp.dot(table_ref[0, rows, :], weighted, preferred_element_type=F32)
        by_imag = jnp.dot(table_ref[1, rows, :], weighted, preferred_element_type=F32)
        out_ref[k, 0] = (before_ref[rows, :half] + (by_real[:, :half] - by_imag[:, half:])).astype(BF16)
        out_ref[k, 1] = (before_ref[rows, half:] + (by_real[:, half:] + by_imag[:, :half])).astype(BF16)
        copies.append(pltpu.make_async_copy(out_ref.at[k], out_hbm.at[:, pl.ds(k * size, size), :], copied.at[k]))
        copies[-1].start()
    for copy in copies:
        copy.wait()


def back_last(table, weighted, before):
    gcount, width = before.shape
    return pl.pallas_call(
        back_last_kernel,
        out_shape=jax.ShapeDtypeStruct((2, gcount, width // 2), BF16),
        in_specs=[vmem()] * 3, out_specs=hbm(),
        scratch_shapes=[pltpu.VMEM((CHUNKS, 2, gcount // CHUNKS, width // 2), BF16),
                        pltpu.SemaphoreType.DMA((CHUNKS,))],
        compiler_params=LIMIT, name="back_last",
    )(table, weighted, before)


def farthest_first(places, extents, first):
    def distance(i):
        steps = [abs(a - b) for a, b in zip(places[i], places[first])]
        return sum(min(s, n - s) for s, n in zip(steps, extents))
    others = [i for i in range(len(places)) if i != first]
    return [first] + sorted(others, key=lambda i: (-distance(i), (i - first) % len(places)))


def exchange(blocks, axis, members):
    return lax.all_to_all(blocks, axis, 0, 0, axis_index_groups=[members], tiled=True)


def local(wavefunctions, miller, reciprocal, fractional, species, atom_order, radial_widths,
          onsite_base, coupling, occupations):
    chips = lax.axis_size("chip")
    bands = lax.axis_size("band")
    swap = [(0, 1), (1, 0)]
    nb = wavefunctions.shape[2]
    owners = farthest_first([(i // 2, i % 2 * 2) for i in range(chips)], (chips // 2, 4), chips * 3 // 4 + 1)
    blocks = farthest_first([(i % (bands // 2), i * 2 // bands) for i in range(bands)], (bands // 2, 4), bands * 3 // 4 + 1)
    other, other_proj, own_row, grid, rhs = other_tables(
        owners, wavefunctions, miller, reciprocal, fractional, species, atom_order, radial_widths)
    received = lax.ppermute(other_proj, "core", swap)
    mine, mine_proj, couple, base_rows, weights = own_tables(
        bands, owners, own_row, grid, rhs, onsite_base, coupling, occupations.reshape(1, -1))
    chip_sum = (mine_proj + received.astype(F32)).astype(BF16).reshape(chips, -1, 2 * nb)
    parts = exchange(chip_sum, "chip", owners)

    proj, occupancy = occupancy_step(parts, weights, bands)
    occupancy = exchange(occupancy, "band", blocks)
    onsite, weighted = weigh(occupancy, proj, couple, base_rows, chips)
    weighted = exchange(weighted, "chip", owners).reshape(-1, 2 * nb)
    other_weighted = lax.ppermute(weighted, "core", swap)
    before, other_t, onsite = back(mine, weighted, other, onsite)
    applied = back_last(other_t, other_weighted, before)
    return applied, onsite


def solution(mesh):
    peers, bands = mesh.devices.shape
    inner = Mesh(mesh.devices.reshape(peers // 2, 2, bands), ("chip", "core", "band"))
    pw = ("chip", "core")
    placed = (P(None, pw, "band"), P(None, pw), P(), P(), P(), P(), P(), P(), P(), P("band"))
    return jax.shard_map(
        local,
        mesh=inner,
        in_specs=placed,
        out_specs=(P(None, pw, "band"), P(pw, None, None)),
        check_vma=False,
    )
```

```python
import functools
import math

import jax
import jax.numpy as jnp
from jax import lax
from jax.experimental import pallas as pl
from jax.experimental.pallas import tpu as pltpu
from jax.sharding import Mesh
from jax.sharding import PartitionSpec as P

HIGH = lax.Precision.HIGHEST
F32 = jnp.float32
BF16 = jnp.bfloat16
OTHER_ENDS = (10, 14, 16)
OWN_ENDS = (16,)
CHUNKS = 4
SIN = (6.283185005187988, -41.341590881347656, 81.59994506835938,
       -76.61447143554688, 41.3428840637207, -12.471243858337402)
COS = (1.0, -19.73920440673828, 64.93911743164062, -85.45014190673828,
       60.16762924194336, -25.967599868774414, 6.528658390045166)
NT = (((1,), (1,)), ((), ()))
TN = (((0,), (0,)), ((), ()))
NN = (((1,), (0,)), ((), ()))


LIMIT = pltpu.CompilerParams(vmem_limit_bytes=16 << 20)


def dot_high(left, right, dims):
    return lax.dot_general(left, right, dims, precision=HIGH, preferred_element_type=F32)


def iota(shape, dim):
    return lax.broadcasted_iota(jnp.int32, shape, dim)


def in_parts(array):
    high = array.astype(BF16).astype(F32)
    rest = array - high
    middle = rest.astype(BF16).astype(F32)
    return high, middle, rest - middle


def gather_lanes(array, order):
    rows, lanes = array.shape
    parts = jnp.concatenate(in_parts(array), axis=0).astype(BF16)
    chosen = (iota((lanes, lanes), 0) == order).astype(F32).astype(BF16)
    picked = jnp.dot(parts, chosen, preferred_element_type=F32)
    return picked[:rows] + picked[rows:2 * rows] + picked[2 * rows:]


def horner(coefficients, z):
    total = jnp.full_like(z, coefficients[-1])
    for c in coefficients[-2::-1]:
        total = total * z + c
    return total


def vmem():
    return pl.BlockSpec(memory_space=pltpu.VMEM)


def hbm():
    return pl.BlockSpec(memory_space=pltpu.HBM)


def in_hbm(array):
    return pltpu.with_memory_space_constraint(array, pltpu.HBM)


def fetch(pairs, copied):
    copies = [pltpu.make_async_copy(src, dst, copied.at[k]) for k, (src, dst) in enumerate(pairs)]
    for copy in copies:
        copy.start()
    return copies


def project_rows(owners, by_row, grid_ref, rhs_ref, beta_ref, proj_ref, ends, before_first):
    done = 0
    gcount = grid_ref.shape[1]
    wide = (8, gcount)
    m, g = ([jnp.broadcast_to(grid_ref[d:d + 1, :], wide) for d in dims] for dims in ((0, 1, 2), (3, 4, 5)))
    g2 = jnp.broadcast_to(grid_ref[6:7, :], wide)
    first = iota(wide, 0) < 4
    pair_g = (None, jnp.where(first, g[0], g[1]), jnp.where(first, g[2], g[0]), jnp.where(first, g[1], g[2]))
    first1 = iota((8, 1), 0) < 4
    for q, chip in enumerate(owners):
        par = by_row[chip * 8:chip * 8 + 8, :]
        if q % 2 == 0:
            here = [par[:, k:k + 1] for k in range(3)]
            after = by_row[owners[q + 1] * 8:owners[q + 1] * 8 + 8, :]
            spot = [jnp.where(first1, here[k], after[:, k:k + 1]) for k in range(3)]
            turns = spot[0] * m[0] + spot[1] * m[1] + spot[2] * m[2]
            r = turns - jnp.round(turns)
            z = r * r
            both = [(v, pltpu.roll(v, 4, 0)) for v in (horner(SIN, z) * r, horner(COS, z))]
            sin, cos = (jnp.where(first, v, turned) for v, turned in both)
        else:
            sin, cos = (jnp.where(first, turned, v) for v, turned in both)
        minus_sin = -sin
        col = [par[:, k:k + 1] for k in range(7)]
        pair_w = (jnp.where(first1, col[3], col[4]), col[5], jnp.where(first1, col[5], col[6]), col[6])
        re, im = [], []
        for p in range(4):
            w = pair_w[p]
            decay = jnp.exp(g2 * (-0.5 * (w * w)))
            if p == 0:
                re.append(decay * cos)
                im.append(decay * minus_sin)
            else:
                amp = pair_g[p] * ((-w) * decay)
                re.append(amp * sin)
                im.append(amp * cos)
        beta_ref[q * 32:q * 32 + 32, 0:gcount] = jnp.concatenate(re, axis=0).astype(BF16)
        beta_ref[q * 32:q * 32 + 32, gcount:] = jnp.concatenate(im, axis=0).astype(BF16)
        if q + 1 in ends:
            if done == 0:
                before_first()
            rows = slice(done * 32, (q + 1) * 32)
            by_real = jnp.dot(beta_ref[rows, :gcount], rhs_ref[...], preferred_element_type=F32)
            by_imag = jnp.dot(beta_ref[rows, gcount:], rhs_ref[...], preferred_element_type=F32)
            half = rhs_ref.shape[1] // 2
            proj_ref[rows, :half] = (by_real[:, :half] + by_imag[:, half:]).astype(proj_ref.dtype)
            proj_ref[rows, half:] = (by_real[:, half:] - by_imag[:, :half]).astype(proj_ref.dtype)
            done = q + 1


def other_tables_kernel(owners, recip_hbm, widths_hbm, wave_hbm, miller_hbm, frac_hbm, species_hbm, order_hbm,
                        beta_ref, proj_ref, own_row_ref, grid_ref, rhs_ref,
                        recip_ref, widths_ref, wave_ref, miller_ref, frac_ref, species_ref, order_ref, copied):
    *loads, wave_load = fetch(
        ((order_hbm, order_ref), (species_hbm, species_ref), (widths_hbm, widths_ref), (frac_hbm, frac_ref),
         (recip_hbm, recip_ref), (miller_hbm, miller_ref), (wave_hbm, wave_ref)), copied)
    for load in loads:
        load.wait()
    core = lax.axis_index("core")
    gcount = miller_ref.shape[1]
    natoms = order_ref.shape[1]
    kinds = widths_ref.shape[0]
    spec = species_ref[...]
    rows = [frac_ref[d:d + 1, :] for d in range(3)]
    for c in range(4):
        row = jnp.zeros((1, natoms), F32)
        for s in range(kinds):
            row = jnp.where(spec == s, widths_ref[s:s + 1, c:c + 1], row)
        rows.append(row)
    rows.append(spec.astype(F32))
    by_slot = gather_lanes(jnp.concatenate(rows, axis=0), order_ref[...]).T
    low = iota((8, 8), 0) < 4
    first_four, last_four = [], []
    for q in range(len(owners)):
        here = by_slot[q * 8:q * 8 + 8, :]
        turned = pltpu.roll(here, 4, 0)
        first_four.append(jnp.where(low, here, turned))
        last_four.append(jnp.where(low, turned, here))
    first_four = jnp.concatenate(first_four, axis=0)
    last_four = jnp.concatenate(last_four, axis=0)
    by_row = jnp.where(core == 0, last_four, first_four)
    own_row_ref[...] = jnp.where(core == 0, first_four, last_four)

    mil = miller_ref[...].astype(F32)
    m = [mil[d:d + 1, :] for d in range(3)]
    two_pi = 2.0 * math.pi
    g = [two_pi * (recip_ref[d:d + 1, 0:1] * m[0] + recip_ref[d:d + 1, 1:2] * m[1] + recip_ref[d:d + 1, 2:3] * m[2])
         for d in range(3)]
    g2 = g[0] * g[0] + g[1] * g[1] + g[2] * g[2]
    grid_ref[...] = jnp.concatenate([*m, *g, g2, g2], axis=0)

    def make_rhs():
        wave_load.wait()
        nb = wave_ref.shape[2]
        rhs_ref[:, :nb] = wave_ref[0]
        rhs_ref[:, nb:] = wave_ref[1]

    project_rows(owners, by_row, grid_ref, rhs_ref, beta_ref, proj_ref, OTHER_ENDS, make_rhs)


def other_tables(owners, wavefunctions, miller, reciprocal, fractional, species, atom_order, radial_widths):
    gcount, nb = wavefunctions.shape[1:]
    natoms = atom_order.shape[0]
    args = (reciprocal, radial_widths, wavefunctions, miller, fractional, species.reshape(1, -1),
            atom_order.reshape(1, -1))
    return pl.pallas_call(
        functools.partial(other_tables_kernel, owners),
        out_shape=(jax.ShapeDtypeStruct((natoms * 4, 2 * gcount), BF16),
                   jax.ShapeDtypeStruct((natoms * 4, 2 * nb), BF16),
                   jax.ShapeDtypeStruct((natoms, 8), F32), jax.ShapeDtypeStruct((8, gcount), F32),
                   jax.ShapeDtypeStruct((gcount, 2 * nb), BF16)),
        in_specs=[hbm()] * len(args),
        out_specs=(vmem(),) * 5,
        scratch_shapes=[pltpu.VMEM(a.shape, a.dtype) for a in args] + [pltpu.SemaphoreType.DMA((len(args),))],
        compiler_params=LIMIT,
        name="other_tables",
    )(*(in_hbm(a) for a in args))


def own_tables_kernel(bands, owners, own_row_ref, grid_ref, rhs_ref, base_ref, coupling_hbm, occupations_hbm,
                      beta_ref, proj_ref, couple_ref, base_rows_ref, weights_ref,
                      coupling_ref, occupations_ref, copied):
    loads = fetch(((coupling_hbm, coupling_ref), (occupations_hbm, occupations_ref)), copied)
    chip = lax.axis_index("chip")

    def of_owned_atoms():
        for load in loads:
            load.wait()
        spec = own_row_ref[pl.ds(pl.multiple_of(chip * 8, 8), 8), 7:8]
        kinds = base_ref.shape[0]
        base = jnp.broadcast_to(base_ref[0:1, :], (8, 64))
        for s in range(1, kinds):
            base = jnp.where(spec == s, base_ref[s:s + 1, :], base)
        base_rows_ref[...] = base
        by_kind = [coupling_ref[s].T for s in range(kinds)]
        for a in range(4):
            for i in range(8):
                rows = slice(i * 8, i * 8 + 8)
                block = by_kind[0][rows]
                for s in range(1, kinds):
                    block = jnp.where(spec[a:a + 1, :] == s, by_kind[s][rows], block)
                to = ((i % 2) * 4 + i // 2) * 32 + a * 8
                couple_ref[to:to + 8, :] = block
        w = occupations_ref[...] * (1.0 / (occupations_ref.shape[1] * bands))
        weights_ref[...] = jnp.concatenate([w, w], axis=1)

    project_rows(owners, own_row_ref[...], grid_ref, rhs_ref, beta_ref, proj_ref, OWN_ENDS, of_owned_atoms)


def own_tables(bands, owners, own_row, grid, rhs, base, coupling, occupations):
    nrows = own_row.shape[0] * 4
    return pl.pallas_call(
        functools.partial(own_tables_kernel, bands, owners),
        out_shape=(jax.ShapeDtypeStruct((nrows, 2 * rhs.shape[0]), BF16), jax.ShapeDtypeStruct((nrows, rhs.shape[1]), F32),
                   jax.ShapeDtypeStruct((256, 64), F32), jax.ShapeDtypeStruct((8, 64), F32),
                   jax.ShapeDtypeStruct((1, rhs.shape[1]), F32)),
        in_specs=[vmem()] * 4 + [hbm()] * 2,
        out_specs=(vmem(),) * 5,
        scratch_shapes=[pltpu.VMEM(coupling.shape, F32), pltpu.VMEM(occupations.shape, F32),
                        pltpu.SemaphoreType.DMA((2,))],
        compiler_params=LIMIT,
        name="own_tables",
    )(own_row, grid, rhs, base, in_hbm(coupling), in_hbm(occupations))


def occupancy_kernel(parts_ref, weights_ref, proj_ref, send_ref):
    total = parts_ref[0].astype(F32)
    for k in range(1, parts_ref.shape[0]):
        total = total + parts_ref[k].astype(F32)
    nb = proj_ref.shape[2]
    proj_ref[0] = total[:, :nb]
    proj_ref[1] = total[:, nb:]
    by_atom = jnp.concatenate([jnp.concatenate(
        [proj_ref[h, pl.ds(a, 8, stride=4), :] for a in range(4)], axis=0) for h in range(2)], axis=1)
    gram = dot_high(total * weights_ref[...], by_atom, NT)
    flat = jnp.concatenate([gram[k * 8:k * 8 + 8, :] for k in range(4)], axis=1)
    flat = jnp.where((iota((8, 128), 1) // 8) % 4 == iota((8, 128), 0) % 4, flat, 0.0)
    flat = flat + pltpu.roll(flat, 1, 0)
    flat = flat + pltpu.roll(flat, 2, 0)
    flat = jnp.concatenate([flat[3:4, :], flat[7:8, :]], axis=0)
    for k in range(send_ref.shape[0]):
        send_ref[k] = flat


def occupancy_step(parts, weights, peers):
    _, nrows, width = parts.shape
    return pl.pallas_call(
        occupancy_kernel,
        out_shape=(jax.ShapeDtypeStruct((2, nrows, width // 2), F32), jax.ShapeDtypeStruct((peers, 2, 128), F32)),
        in_specs=[vmem(), vmem()],
        out_specs=(vmem(), vmem()),
        compiler_params=LIMIT,
        name="occupancy",
    )(parts, weights)


def weigh_kernel(parts_ref, proj_ref, couple_ref, base_ref, onsite_ref, send_ref):
    occ = parts_ref[0]
    for k in range(1, parts_ref.shape[0]):
        occ = occ + parts_ref[k]
    occ = jnp.concatenate([occ[0:1, :], occ[1:2, :]], axis=1)
    own_atom = (iota((8, 256), 1) // 8) % 4 == iota((8, 256), 0) % 4
    onsite = dot_high(jnp.where(own_atom, occ, 0.0), couple_ref[...], NN) + base_ref[...]
    onsite_ref[...] = onsite
    pair = jnp.where(iota((8, 64), 0) < 4, onsite, jnp.concatenate([onsite[:, 8:], onsite[:, :8]], axis=1))
    low = iota((8, 2 * proj_ref.shape[2]), 0) < 4
    total = [None] * 4
    for k in range(4):
        here = jnp.concatenate([proj_ref[h, k * 8:k * 8 + 8, :] for h in range(2)], axis=1)
        turned = pltpu.roll(here, 4, 0)
        for j, both in ((2 * k, jnp.where(low, here, turned)), (2 * k + 1, jnp.where(low, turned, here))):
            for t in range(4):
                term = pair[:, 16 * t + j:16 * t + j + 1] * both
                total[t] = term if total[t] is None else total[t] + term
    weighted = jnp.concatenate(total, axis=0).astype(BF16)
    for k in range(send_ref.shape[0]):
        send_ref[k] = weighted


def weigh(parts, proj, couple, base_rows, peers):
    return pl.pallas_call(
        weigh_kernel,
        out_shape=(jax.ShapeDtypeStruct((8, 64), F32), jax.ShapeDtypeStruct((peers, proj.shape[1], 2 * proj.shape[2]), BF16)),
        in_specs=[vmem()] * 4,
        out_specs=(vmem(), vmem()),
        compiler_params=LIMIT,
        name="weigh",
    )(parts, proj, couple, base_rows)


def turned_by_i(weighted):
    half = weighted.shape[1] // 2
    return jnp.concatenate([-weighted[:, half:], weighted[:, :half]], axis=1)


def back_kernel(table_ref, weighted_ref, other_ref, onsite_ref, out_ref, other_t_ref, square_ref):
    for i in range(8):
        square_ref[:, i, :] = onsite_ref[0:4, i * 8:i * 8 + 8]
    gcount = table_ref.shape[1] // 2
    weighted = weighted_ref[...]
    total = (lax.dot_general(weighted, table_ref[:, :gcount], TN, preferred_element_type=F32)
             + lax.dot_general(turned_by_i(weighted), table_ref[:, gcount:], TN, preferred_element_type=F32))
    out_ref[...] = total.T
    other_t_ref[0] = other_ref[:, :gcount].T
    other_t_ref[1] = other_ref[:, gcount:].T


def back(table, weighted, other, onsite):
    gcount = table.shape[1] // 2
    return pl.pallas_call(
        back_kernel,
        out_shape=(jax.ShapeDtypeStruct((gcount, weighted.shape[1]), F32),
                   jax.ShapeDtypeStruct((2, gcount, other.shape[0]), BF16), jax.ShapeDtypeStruct((4, 8, 8), F32)),
        in_specs=[vmem()] * 4, out_specs=(vmem(),) * 3, compiler_params=LIMIT, name="back",
    )(table, weighted, other, onsite)


def back_last_kernel(table_ref, weighted_ref, before_ref, out_hbm, out_ref, copied):
    half = weighted_ref.shape[1] // 2
    weighted = weighted_ref[...]
    chunks = copied.shape[0]
    size = table_ref.shape[1] // chunks
    copies = []
    for k in range(chunks):
        rows = slice(k * size, (k + 1) * size)
        by_real = jnp.dot(table_ref[0, rows, :], weighted, preferred_element_type=F32)
        by_imag = jnp.dot(table_ref[1, rows, :], weighted, preferred_element_type=F32)
        out_ref[k, 0] = (before_ref[rows, :half] + (by_real[:, :half] - by_imag[:, half:])).astype(BF16)
        out_ref[k, 1] = (before_ref[rows, half:] + (by_real[:, half:] + by_imag[:, :half])).astype(BF16)
        copies.append(pltpu.make_async_copy(out_ref.at[k], out_hbm.at[:, pl.ds(k * size, size), :], copied.at[k]))
        copies[-1].start()
    for copy in copies:
        copy.wait()


def back_last(table, weighted, before):
    gcount, width = before.shape
    return pl.pallas_call(
        back_last_kernel,
        out_shape=jax.ShapeDtypeStruct((2, gcount, width // 2), BF16),
        in_specs=[vmem()] * 3, out_specs=hbm(),
        scratch_shapes=[pltpu.VMEM((CHUNKS, 2, gcount // CHUNKS, width // 2), BF16),
                        pltpu.SemaphoreType.DMA((CHUNKS,))],
        compiler_params=LIMIT, name="back_last",
    )(table, weighted, before)


def farthest_first(places, extents, first):
    def distance(i):
        steps = [abs(a - b) for a, b in zip(places[i], places[first])]
        return sum(min(s, n - s) for s, n in zip(steps, extents))
    others = [i for i in range(len(places)) if i != first]
    return [first] + sorted(others, key=lambda i: (-distance(i), (i - first) % len(places)))


def exchange(blocks, axis, members):
    return lax.all_to_all(blocks, axis, 0, 0, axis_index_groups=[members], tiled=True)


def local(wavefunctions, miller, reciprocal, fractional, species, atom_order, radial_widths,
          onsite_base, coupling, occupations):
    chips = lax.axis_size("chip")
    bands = lax.axis_size("band")
    swap = [(0, 1), (1, 0)]
    nb = wavefunctions.shape[2]
    owners = farthest_first([(i // 2, i % 2 * 2) for i in range(chips)], (chips // 2, 4), chips * 3 // 4 + 1)
    blocks = farthest_first([(i % (bands // 2), i * 2 // bands) for i in range(bands)], (bands // 2, 4), bands * 3 // 4 + 1)
    other, other_proj, own_row, grid, rhs = other_tables(
        owners, wavefunctions, miller, reciprocal, fractional, species, atom_order, radial_widths)
    received = lax.ppermute(other_proj, "core", swap)
    mine, mine_proj, couple, base_rows, weights = own_tables(
        bands, owners, own_row, grid, rhs, onsite_base.reshape(-1, 64), coupling, occupations.reshape(1, -1))
    chip_sum = (mine_proj + received.astype(F32)).astype(BF16).reshape(chips, -1, 2 * nb)
    parts = exchange(chip_sum, "chip", owners)

    proj, occupancy = occupancy_step(parts, weights, bands)
    occupancy = exchange(occupancy, "band", blocks)
    onsite, weighted = weigh(occupancy, proj, couple, base_rows, chips)
    weighted = exchange(weighted, "chip", owners).reshape(-1, 2 * nb)
    other_weighted = lax.ppermute(weighted, "core", swap)
    before, other_t, onsite = back(mine, weighted, other, onsite)
    applied = back_last(other_t, other_weighted, before)
    return applied, onsite


def solution(mesh):
    peers, bands = mesh.devices.shape
    inner = Mesh(mesh.devices.reshape(peers // 2, 2, bands), ("chip", "core", "band"))
    pw = ("chip", "core")
    placed = (P(None, pw, "band"), P(None, pw), P(), P(), P(), P(), P(), P(), P(), P("band"))
    return jax.shard_map(
        local,
        mesh=inner,
        in_specs=placed,
        out_specs=(P(None, pw, "band"), P(pw, None, None)),
        check_vma=False,
    )
```
